32 devices in a mesh: field: 8 (over y, x, core), point: 4 (over z).
Axes of the slice: x: 2, y: 2, z: 4, core: 2. Of those that a mesh axis runs over, the one named last changes fastest.
Arguments:
- residual_in: bfloat16 [8, 1024, 2048], P('field', 'point'), may hold values from -6 to 6
- coefs_in: bfloat16 [8, 1024, 4, 256], P('field', 'point'), may hold values from 0 to 1
- dictionary: bfloat16 [2048, 2048], P('field'), may hold values from -0.125 to 0.125
- owner_order: int32 [8], replicated, may hold values from 0 to 7, each once
- pixel_of: int32 [8, 1024], P('field', 'point'), may hold values from 0 to 1023, each once within a row
Outputs:
- maps: float32 [8, 4, 256, 8, 128], P('field', None, 'point')
The draws below stay inside these ranges and needn't reach their ends.
Inputs may be any that keep to these rules, and one draw needn't show every extreme that they name: `owner_order`: A permutation of the dictionary blocks. `pixel_of`: each field's row is a permutation of its scan points over the 8 x 128 pixels.
All inputs are finite; a program needn't handle non-finite values.
Results may differ from the reference program's by a relative error of at most 0.00045.
Values may be sent and summed in bfloat16 or wider, within the bound.
No kernel may reach another device: no remote copies, remote signals or barrier semaphores. Data moves between devices by JAX's collectives and lax.ppermute only.
A program may use at most 64 MiB of HBM per device.

```python
import jax
import jax.numpy as jnp
from jax import lax

F = 2048
KB = 256
TURNS = 4
SWEEPS = 4
MAP_W = 128
NPTS = 1024
TEMPLATES = 2048
N_FIELD = 8


def shard_levels(stream_key, shape, cuts, smallest, high):
    def one(position, parts):
        heights = jax.random.uniform(jax.random.fold_in(jax.random.fold_in(stream_key, 6), position), (parts,), jnp.float32, smallest / len(cuts), high / len(cuts))
        return jnp.repeat(jnp.exp(heights), shape[position] // parts).reshape((-1,) + (1,) * (len(shape) - position - 1))

    gain = one(*cuts[0])
    for cut in cuts[1:]:
        gain = gain * one(*cut)
    return gain


def bell_draw(stream_key, shape, deviation, bound, pieces=(), dtype=jnp.bfloat16):
    entries = deviation * jax.random.normal(stream_key, shape, jnp.float32)
    if pieces:
        entries = entries * shard_levels(stream_key, shape, pieces, -0.22, 0.18)
    return jnp.clip(entries, -bound, bound).astype(dtype)


def setup_inputs(seed: int = 0) -> dict:
    splits = jax.random.split(jax.random.key(seed), 6)
    residual_in = bell_draw(splits[0], (N_FIELD, NPTS, F), 1.0, 6.0, ((0, 8), (1, 4)))
    coefs_in = jnp.clip(1.0 * jax.random.uniform(splits[1], (N_FIELD, NPTS, TURNS, KB), jnp.float32) ** shard_levels(splits[1], (N_FIELD, NPTS, TURNS, KB), ((0, 8), (1, 4)), -0.2, 0.2), 0.0, 1.0).astype(jnp.bfloat16)
    dictionary = bell_draw(splits[2], (TEMPLATES, F), F ** -0.5, 0.125, ((0, 8),))
    owner_order = jax.random.permutation(splits[3], N_FIELD).astype(jnp.int32)
    pixel_of = jax.vmap(lambda own: jax.random.permutation(own, NPTS))(jax.random.split(splits[4], N_FIELD)).reshape((N_FIELD, NPTS)).astype(jnp.int32)
    return {"residual_in": residual_in, "coefs_in": coefs_in, "dictionary": dictionary, "owner_order": owner_order, "pixel_of": pixel_of}


time_step = 0.2
edge_scale = 0.5


def block_steps(templates):
    gram = lax.dot_general(templates, templates, (((1,), (1,)), ((), ())), preferred_element_type=jnp.float32)
    return 1.0 / jnp.sum(jnp.abs(gram), axis=1)


def diffuse(grids):
    for repeat in range(SWEEPS):
        padded = jnp.pad(grids, ((0, 0), (1, 1), (1, 1)), mode="edge")
        summed = jnp.zeros_like(grids)
        for neighbour in (padded[:, :-2, 1:-1], padded[:, 2:, 1:-1], padded[:, 1:-1, :-2], padded[:, 1:-1, 2:]):
            differ = neighbour - grids
            scaled = differ / edge_scale
            summed = summed + differ / (1.0 + scaled * scaled)
        grids = grids + time_step * summed
    return grids


def reference(residual_in, coefs_in, dictionary, owner_order, pixel_of):
    blocks = dictionary.reshape(N_FIELD, KB, F)
    chosen = []
    steps_all = []
    for turn_index in range(TURNS):
        templates = blocks[owner_order[turn_index]]
        chosen.append(templates)
        steps_all.append(block_steps(templates))

    def one_field(inputs):
        residual, coefs, pixel_ids = inputs
        coefs = coefs.astype(jnp.float32)
        updated = []
        for turn_index in range(TURNS):
            templates = chosen[turn_index]
            correlation = lax.dot_general(residual, templates, (((1,), (1,)), ((), ())), preferred_element_type=jnp.float32)
            before = coefs[:, turn_index, :]
            after = jnp.maximum(before + steps_all[turn_index][None, :] * correlation, 0.0)
            updated.append(after)
            if turn_index + 1 < TURNS:
                change = (after - before).astype(jnp.bfloat16)
                residual = (residual.astype(jnp.float32) - jnp.dot(change, templates, preferred_element_type=jnp.float32)).astype(jnp.bfloat16)
        stacked = jnp.stack(updated, axis=1)
        values = stacked.reshape(NPTS, TURNS * KB).T
        flat = jnp.zeros((TURNS * KB, NPTS), jnp.float32).at[:, pixel_ids].set(values)
        grids = diffuse(flat.reshape(TURNS * KB, NPTS // MAP_W, MAP_W))
        return grids.reshape(TURNS, KB, NPTS // MAP_W, MAP_W)

    return lax.map(one_field, (residual_in, coefs_in, pixel_of))
```

```python
import functools

import jax
import jax.numpy as jnp
from jax import lax
from jax.experimental import pallas as pl
from jax.experimental.pallas import tpu as pltpu
from jax.sharding import PartitionSpec as P

TURNS = 4
SWEEPS = 4
MAP_W = 128
SUBLANES = 8
PARTS = 3

time_step = 0.2

GROUPS = ((0, 1), (2, 3))

ANY = pl.BlockSpec(memory_space=pl.ANY)
VMEM = pl.BlockSpec(memory_space=pltpu.VMEM)
SMEM = pl.BlockSpec(memory_space=pltpu.SMEM)


def place_of_device():
    index = lax.axis_index("field")
    return index // 2, index % 2


def slice_kernel(chips, block_ref, *refs):
    keep, give, sems = refs[:chips], refs[chips : 2 * chips], refs[2 * chips]
    chip, core = place_of_device()
    rows, half = keep[0].shape
    copies = []
    for k in range(chips):
        top = pl.multiple_of((chip ^ k) * rows, rows)
        for number, (out, which) in enumerate(((give[k], 1 - core), (keep[k], core))):
            left = pl.multiple_of(which * half, half)
            copy = pltpu.make_async_copy(
                block_ref.at[pl.ds(top, rows), pl.ds(left, half)], out, sems.at[2 * k + number]
            )
            copy.start()
            copies.append(copy)
    for copy in copies:
        copy.wait()


def cut_block(block, chips):
    kb, features = block.shape
    piece = jax.ShapeDtypeStruct((kb // chips, features // 2), block.dtype)
    outs = pl.pallas_call(
        functools.partial(slice_kernel, chips),
        out_shape=[piece] * (2 * chips),
        in_specs=[ANY],
        out_specs=[VMEM] * (2 * chips),
        scratch_shapes=[pltpu.SemaphoreType.DMA((2 * chips,))],
        name="cut",
    )(block)
    return outs[:chips], outs[chips:]


def pick_kernel(chips, order_ref, *refs):
    same, other = refs[:chips], refs[chips : 2 * chips]
    outs, sems = refs[2 * chips : 2 * chips + TURNS], refs[2 * chips + TURNS]
    chip, core = place_of_device()
    for turn in range(TURNS):
        owner = order_ref[turn]
        distance = (owner // 2) ^ chip
        mine = owner % 2 == core
        for k in range(chips):

            @pl.when((distance == k) & mine)
            def _():
                pltpu.make_async_copy(same[k], outs[turn], sems.at[turn]).start()

            @pl.when((distance == k) & jnp.logical_not(mine))
            def _():
                pltpu.make_async_copy(other[k], outs[turn], sems.at[turn]).start()

    for turn in range(TURNS):
        pltpu.make_async_copy(same[0], outs[turn], sems.at[turn]).wait()


def pick_turns(owner_order, same, other):
    chips = len(same)
    piece = jax.ShapeDtypeStruct(same[0].shape, same[0].dtype)
    return pl.pallas_call(
        functools.partial(pick_kernel, chips),
        out_shape=[piece] * TURNS,
        in_specs=[SMEM] + [ANY] * (2 * chips),
        out_specs=[VMEM] * TURNS,
        scratch_shapes=[pltpu.SemaphoreType.DMA((TURNS,))],
        name="pick",
    )(owner_order, *same, *other)


def turn_kernel(turns, chips, parts, last, with_pixels, *refs):
    count = len(turns)
    refs = list(refs)
    residual_ref, coefs_ref = refs.pop(0), refs.pop(0)
    pixel_ref = refs.pop(0) if with_pixels else None
    pieces = [[refs.pop(0) for _ in range(2 * chips)] for _ in turns]
    residual_out = None if last else refs.pop(0)
    sends = [refs.pop(0) for _ in range(parts)]
    blocks, values, held, sems = refs

    chip, core = place_of_device()
    slot = lax.axis_index("point")
    rows, half = pieces[0][0].shape
    kb = rows * chips
    local_kb = kb // parts
    copies = []
    for position in range(count):
        for number, piece in enumerate(pieces[position]):
            k, which = number % chips, number // chips
            top = pl.multiple_of((chip ^ k) * rows, rows)
            left = pl.multiple_of((core if which == 0 else 1 - core) * half, half)
            copy = pltpu.make_async_copy(
                piece,
                blocks.at[position, pl.ds(top, rows), pl.ds(left, half)],
                sems.at[position, number],
            )
            copy.start()
            copies.append((position, copy))

    source = residual_ref
    for position, turn in enumerate(turns):
        for where, copy in copies:
            if where == position:
                copy.wait()
        block = blocks.at[position]
        templates = block[...]
        gram = lax.dot_general(
            templates, templates, (((1,), (1,)), ((), ())), preferred_element_type=jnp.float32
        )
        step = 1.0 / jnp.sum(jnp.abs(gram), axis=0, keepdims=True)
        correlation = lax.dot_general(
            source[...], templates, (((1,), (1,)), ((), ())), preferred_element_type=jnp.float32
        )
        before = coefs_ref[:, turn * kb : (turn + 1) * kb].astype(jnp.float32)
        after = jnp.maximum(before + step * correlation, 0.0)
        if turn + 1 < TURNS:
            change = (after - before).astype(jnp.bfloat16)
            features = 2 * half
            width = features // 4
            target = residual_out if position + 1 == count else held
            for start in range(0, features, width):
                columns = slice(start, start + width)
                moved = jnp.dot(change, block[:, columns], preferred_element_type=jnp.float32)
                target[:, columns] = (source[:, columns].astype(jnp.float32) - moved).astype(
                    jnp.bfloat16
                )
            source = target
        values[...] = after.T
        for m in range(parts):
            top = pl.multiple_of((slot ^ m) * local_kb, local_kb)
            sends[m][position * local_kb : (position + 1) * local_kb, :] = values[
                pl.ds(top, local_kb), :
            ]
    if with_pixels:
        row = jnp.broadcast_to(pixel_ref[...].astype(jnp.float32), (SUBLANES, values.shape[1]))
        for m in range(parts):
            sends[m][count * local_kb :, :] = row


def run_turns(turns, residual, coefs, pixels, pieces, parts):
    count = len(turns)
    last = turns[-1] + 1 == TURNS
    chips = len(pieces[0]) // 2
    rows, half = pieces[0][0].shape
    points, features = residual.shape
    kb = rows * chips
    local_kb = kb // parts
    height = count * local_kb + (SUBLANES if pixels is not None else 0)
    send = jax.ShapeDtypeStruct((height, points), jnp.float32)
    flat = [piece for turn in pieces for piece in turn]
    first = [] if last else [jax.ShapeDtypeStruct(residual.shape, residual.dtype)]
    extra = [] if pixels is None else [pixels]
    flops = count * 2 * kb * features * (kb + 2 * points)
    outs = pl.pallas_call(
        functools.partial(turn_kernel, turns, chips, parts, last, pixels is not None),
        out_shape=first + [send] * parts,
        in_specs=[VMEM, VMEM] + [VMEM] * len(extra) + [ANY] * len(flat),
        out_specs=[VMEM] * (len(first) + parts),
        scratch_shapes=[
            pltpu.VMEM((count, kb, features), residual.dtype),
            pltpu.VMEM((kb, points), jnp.float32),
            pltpu.VMEM(residual.shape, residual.dtype),
            pltpu.SemaphoreType.DMA((count, 2 * chips)),
        ],
        cost_estimate=pl.CostEstimate(
            flops=flops, bytes_accessed=2 * features * (2 * points + count * kb), transcendentals=0
        ),
        name="turns_" + str(turns[0]),
    )(residual, coefs, *extra, *flat)
    outs = list(outs)
    return (None if last else outs.pop(0)), outs


def spread(whole):
    rows = len(whole)
    lane = lax.broadcasted_iota(jnp.int32, whole[0].shape, 1)
    inner = lane < MAP_W - 1

    def flow(differ):
        scaled = differ + differ
        return differ / (1.0 + scaled * scaled)

    down = [flow(whole[r + 1] - whole[r]) for r in range(rows - 1)]
    new = []
    for r in range(rows):
        right = flow(pltpu.roll(whole[r], MAP_W - 1, 1) - whole[r])
        right = jnp.where(inner, right, 0.0)
        total = right - pltpu.roll(right, 1, 1)
        if r > 0:
            total = total - down[r - 1]
        if r + 1 < rows:
            total = total + down[r]
        new.append(whole[r] + time_step * total)
    return new


def map_kernel(turns, parts, local_kb, first, *refs):
    count = len(turns)
    refs = list(refs)
    received = [refs.pop(0) for _ in range(parts)]
    pixel_refs = received if first else [refs.pop(0) for _ in range(parts)]
    if not first:
        refs.pop(0)
    out_ref, grids, staged, sem = refs
    rows = grids.shape[0]
    height = count * local_kb
    pieces = []
    for m in range(parts):
        left = received[m][:height, :]
        columns = []
        for part in range(PARTS):
            top = left.astype(jnp.bfloat16)
            columns.append(top)
            if part + 1 < PARTS:
                left = left - top.astype(jnp.float32)
        pieces.append(jnp.concatenate(columns, axis=0))
    values = jnp.concatenate(pieces, axis=1)
    depth = pixel_refs[0].shape[0]
    targets = jnp.concatenate([ref[depth - 1 : depth, :] for ref in pixel_refs], axis=1)
    targets = targets.astype(jnp.int32)
    pixel = lax.broadcasted_iota(jnp.int32, (MAP_W, targets.shape[1]), 0)
    for r in range(rows):
        chosen = jnp.where(pixel == targets - r * MAP_W, 1.0, 0.0).astype(jnp.bfloat16)
        moved = lax.dot_general(
            values, chosen, (((1,), (1,)), ((), ())), preferred_element_type=jnp.float32
        )
        total = moved[:height]
        for part in range(1, PARTS):
            total = total + moved[part * height : (part + 1) * height]
        grids[r] = total

    def one(group, carry):
        top = pl.multiple_of(group * SUBLANES, SUBLANES)
        whole = [grids[r, pl.ds(top, SUBLANES), :] for r in range(rows)]
        for _ in range(SWEEPS):
            whole = spread(whole)
        for r in range(rows):
            staged[pl.ds(group * (SUBLANES * rows) + r, SUBLANES, stride=rows), :] = whole[r]
        return carry

    lax.fori_loop(0, height // SUBLANES, one, 0)
    copy = pltpu.make_async_copy(staged, out_ref.at[pl.ds(turns[0] * local_kb * rows, height * rows)], sem)
    copy.start()
    copy.wait()


def run_maps(turns, received, pixels, buffer, local_kb):
    parts = len(received)
    points = received[0].shape[1]
    rows = parts * points // MAP_W
    first = buffer is None
    height = len(turns) * local_kb
    extra = [] if first else list(pixels) + [buffer]
    return pl.pallas_call(
        functools.partial(map_kernel, turns, parts, local_kb, first),
        out_shape=jax.ShapeDtypeStruct((TURNS * local_kb * rows, MAP_W), jnp.float32),
        in_specs=[VMEM] * (parts if first else 2 * parts) + ([] if first else [ANY]),
        out_specs=ANY,
        scratch_shapes=[
            pltpu.VMEM((rows, height, MAP_W), jnp.float32),
            pltpu.VMEM((height * rows, MAP_W), jnp.float32),
            pltpu.SemaphoreType.DMA,
        ],
        input_output_aliases={} if first else {2 * parts: 0},
        cost_estimate=pl.CostEstimate(
            flops=2 * PARTS * height * (parts * points) ** 2,
            bytes_accessed=8 * height * parts * points,
            transcendentals=0,
        ),
        name="maps_" + str(turns[0]),
    )(*received, *extra)


def exchange(value, axis, size, distance):
    return lax.ppermute(value, axis, [(i, i ^ distance) for i in range(size)])


def per_device(fields, parts, residual_in, coefs_in, dictionary, owner_order, pixel_of):
    residual = residual_in[0]
    points = residual.shape[0]
    coefs = coefs_in[0].reshape(points, -1)
    kb = dictionary.shape[0]
    local_kb = kb // parts
    chips = fields // 2
    over_chips = lambda value, k: exchange(value, "field", fields, 2 * k)
    over_cores = lambda value: exchange(value, "field", fields, 1)

    give, keep = None, None
    keep, give = cut_block(dictionary, chips)
    got = [over_cores(value) for value in give]
    same = [keep[0]] + [over_chips(keep[k], k) for k in range(1, chips)]
    other = [got[0]] + [over_chips(got[k], k) for k in range(1, chips)]
    chosen = pick_turns(owner_order, same, other)

    def gather(turn):
        held = [chosen[turn]]
        for k in range(1, chips):
            low = k & -k
            high = 1 << (k.bit_length() - 1)
            bit = high if turn % 2 == 0 else low
            held.append(over_chips(held[k ^ bit], bit))
        return held + [over_cores(value) for value in held]

    pixels = pixel_of.reshape(1, points)
    buffer, ids = None, None
    for turns in GROUPS:
        pieces = [gather(turn) for turn in turns]
        first = buffer is None
        residual, sends = run_turns(turns, residual, coefs, pixels if first else None, pieces, parts)
        received = [sends[0]] + [exchange(sends[m], "point", parts, m) for m in range(1, parts)]
        if first:
            ids = received
        buffer = run_maps(turns, received, ids, buffer, local_kb)
    rows = parts * points // MAP_W
    return buffer.reshape(1, TURNS, local_kb, rows, MAP_W)


def solution(mesh):
    placed = (
        P("field", "point", None),
        P("field", "point", None, None),
        P("field", None),
        P(),
        P("field", "point"),
    )
    return jax.shard_map(
        functools.partial(per_device, mesh.shape["field"], mesh.shape["point"]),
        mesh=mesh,
        in_specs=placed,
        out_specs=P("field", None, "point", None, None),
        check_vma=False,
    )
```

```python
import functools

import jax
import jax.numpy as jnp
from jax import lax
from jax.experimental import pallas as pl
from jax.experimental.pallas import tpu as pltpu
from jax.sharding import PartitionSpec as P


TURNS = 4
SWEEPS = 4
MAP_W = 128
SUBLANES = 8
UNROLL = 4
TILE_ROWS = 16
GRANT = 16 * 1024 * 1024


time_step = 0.2

GROUPS = ((0, 1), (2, 3))

ANY = pl.BlockSpec(memory_space=pl.ANY)
VMEM = pl.BlockSpec(memory_space=pltpu.VMEM)
SMEM = pl.BlockSpec(memory_space=pltpu.SMEM)


def place_of_device():
    index = lax.axis_index("field")
    return index // 2, index % 2


def slice_kernel(chips, block_ref, *refs):
    keep, give, sems = refs[:chips], refs[chips : 2 * chips], refs[2 * chips]
    chip, core = place_of_device()
    rows, half = keep[0].shape
    copies = []
    for k in range(chips):
        top = pl.multiple_of((chip ^ k) * rows, rows)
        for number, (out, which) in enumerate(((give[k], 1 - core), (keep[k], core))):
            left = pl.multiple_of(which * half, half)
            copy = pltpu.make_async_copy(
                block_ref.at[pl.ds(top, rows), pl.ds(left, half)], out, sems.at[2 * k + number]
            )
            copy.start()
            copies.append(copy)
    for copy in copies:
        copy.wait()


def cut_block(block, chips):
    kb, features = block.shape
    piece = jax.ShapeDtypeStruct((kb // chips, features // 2), block.dtype)
    outs = pl.pallas_call(
        functools.partial(slice_kernel, chips),
        out_shape=[piece] * (2 * chips),
        in_specs=[ANY],
        out_specs=[VMEM] * (2 * chips),
        scratch_shapes=[pltpu.SemaphoreType.DMA((2 * chips,))],
        compiler_params=pltpu.CompilerParams(vmem_limit_bytes=GRANT),
        name="cut",
    )(block)
    return outs[:chips], outs[chips:]


def pick_kernel(chips, order_ref, *refs):
    same, other = refs[:chips], refs[chips : 2 * chips]
    outs, sems = refs[2 * chips : 2 * chips + TURNS], refs[2 * chips + TURNS]
    chip, core = place_of_device()
    for turn in range(TURNS):
        owner = order_ref[turn]
        distance = (owner // 2) ^ chip
        mine = owner % 2 == core
        for k in range(chips):

            @pl.when((distance == k) & mine)
            def _():
                pltpu.make_async_copy(same[k], outs[turn], sems.at[turn]).start()

            @pl.when((distance == k) & jnp.logical_not(mine))
            def _():
                pltpu.make_async_copy(other[k], outs[turn], sems.at[turn]).start()

    for turn in range(TURNS):
        pltpu.make_async_copy(same[0], outs[turn], sems.at[turn]).wait()


def pick_turns(owner_order, same, other):
    chips = len(same)
    piece = jax.ShapeDtypeStruct(same[0].shape, same[0].dtype)
    return pl.pallas_call(
        functools.partial(pick_kernel, chips),
        out_shape=[piece] * TURNS,
        in_specs=[SMEM] + [ANY] * (2 * chips),
        out_specs=[VMEM] * TURNS,
        scratch_shapes=[pltpu.SemaphoreType.DMA((TURNS,))],
        compiler_params=pltpu.CompilerParams(vmem_limit_bytes=GRANT),
        name="pick",
    )(owner_order, *same, *other)


def lay_kernel(parts, coefs_ref, pixel_ref, *refs):
    sends, turned = refs[:parts], refs[parts]
    slot = lax.axis_index("point")
    height, points = sends[0].shape
    local_kb = (height - TILE_ROWS) // TURNS
    turned[...] = coefs_ref[...].astype(jnp.float32).T.astype(jnp.bfloat16)
    pixel = pixel_ref[...]
    half = TILE_ROWS // 2
    row = jnp.broadcast_to((pixel // MAP_W).astype(jnp.float32), (half, points))
    lane = jnp.broadcast_to((pixel % MAP_W).astype(jnp.float32), (half, points))
    both = jnp.concatenate([row, lane], axis=0).astype(jnp.bfloat16)
    for m in range(parts):
        for turn in range(TURNS):
            top = pl.multiple_of((turn * parts + (slot ^ m)) * local_kb, local_kb)
            sends[m][turn * local_kb : (turn + 1) * local_kb, :] = turned[pl.ds(top, local_kb), :]
        sends[m][TURNS * local_kb :, :] = both


def lay_coefs(coefs, pixels, parts):
    points, width = coefs.shape
    send = jax.ShapeDtypeStruct((width // parts + TILE_ROWS, points), jnp.bfloat16)
    outs = pl.pallas_call(
        functools.partial(lay_kernel, parts),
        out_shape=[send] * parts + [jax.ShapeDtypeStruct((width, points), jnp.bfloat16)],
        in_specs=[VMEM, VMEM],
        out_specs=[VMEM] * (parts + 1),
        compiler_params=pltpu.CompilerParams(vmem_limit_bytes=GRANT),
        name="lay",
    )(coefs, pixels)
    return outs[:parts], outs[parts]


def turn_kernel(turns, chips, parts, last, *refs):
    count = len(turns)
    refs = list(refs)
    residual_ref, coefs_ref = refs.pop(0), refs.pop(0)
    pieces = [[refs.pop(0) for _ in range(2 * chips)] for _ in turns]
    residual_out = None if last else refs.pop(0)
    sends = [refs.pop(0) for _ in range(parts)]
    values, held = refs

    chip, core = place_of_device()
    slot = lax.axis_index("point")
    rows, half = pieces[0][0].shape
    kb = rows * chips
    local_kb = kb // parts
    sides = [pl.ds(pl.multiple_of(which * half, half), half) for which in (core, 1 - core)]
    tops = [pl.multiple_of((chip ^ k) * rows, rows) for k in range(chips)]

    source = residual_ref
    for position, turn in enumerate(turns):
        halves = [
            jnp.concatenate([piece[...] for piece in pieces[position][side * chips : (side + 1) * chips]], axis=0)
            for side in range(2)
        ]
        across = lambda left, right: lax.dot_general(
            left, right, (((1,), (1,)), ((), ())), preferred_element_type=jnp.float32
        )
        gram = across(halves[0], halves[0]) + across(halves[1], halves[1])
        step = 1.0 / jnp.sum(jnp.abs(gram), axis=1, keepdims=True)
        correlation = across(halves[0], source[:, sides[0]]) + across(halves[1], source[:, sides[1]])
        before = jnp.concatenate(
            [coefs_ref[pl.ds(pl.multiple_of(turn * kb + top, rows), rows), :] for top in tops], axis=0
        ).astype(jnp.float32)
        after = jnp.maximum(before + step * correlation, 0.0)
        change = (after - before).astype(jnp.bfloat16)
        for k in range(chips):
            values[pl.ds(tops[k], rows), :] = change[k * rows : (k + 1) * rows, :]
        if turn + 1 < TURNS:
            target = residual_out if position + 1 == count else held
            for side, part in zip(sides, halves):
                moved = lax.dot_general(
                    change, part, (((0,), (0,)), ((), ())), preferred_element_type=jnp.float32
                )
                target[:, side] = (source[:, side].astype(jnp.float32) - moved).astype(jnp.bfloat16)
            source = target
        for m in range(parts):
            top = pl.multiple_of((slot ^ m) * local_kb, local_kb)
            sends[m][position * local_kb : (position + 1) * local_kb, :] = values[
                pl.ds(top, local_kb), :
            ]


def run_turns(turns, residual, coefs, pieces, parts):
    count = len(turns)
    last = turns[-1] + 1 == TURNS
    chips = len(pieces[0]) // 2
    rows, _ = pieces[0][0].shape
    points, features = residual.shape
    kb = rows * chips
    local_kb = kb // parts
    send = jax.ShapeDtypeStruct((count * local_kb, points), jnp.bfloat16)
    flat = [piece for turn in pieces for piece in turn]
    first = [] if last else [jax.ShapeDtypeStruct(residual.shape, residual.dtype)]
    flops = count * 2 * kb * features * (kb + 2 * points)
    outs = pl.pallas_call(
        functools.partial(turn_kernel, turns, chips, parts, last),
        out_shape=first + [send] * parts,
        in_specs=[VMEM] * (2 + len(flat)),
        out_specs=[VMEM] * (len(first) + parts),
        scratch_shapes=[
            pltpu.VMEM((kb, points), jnp.bfloat16),
            pltpu.VMEM(residual.shape, residual.dtype),
        ],
        cost_estimate=pl.CostEstimate(
            flops=flops, bytes_accessed=2 * features * (2 * points + count * kb), transcendentals=0
        ),
        compiler_params=pltpu.CompilerParams(vmem_limit_bytes=GRANT),
    )(residual, coefs, *flat)
    outs = list(outs)
    return (None if last else outs.pop(0)), outs


def spread(wholes):
    lane = lax.broadcasted_iota(jnp.int32, wholes[0][0].shape, 1)
    inner = lane < MAP_W - 1

    def flow(differ):
        return differ / (1.0 + differ * differ)

    shifted = [[pltpu.roll(row, MAP_W - 1, 1) for row in whole] for whole in wholes]
    rights = [
        [jnp.where(inner, flow(right - row), 0.0) for row, right in zip(whole, moved)]
        for whole, moved in zip(wholes, shifted)
    ]
    lefts = [[pltpu.roll(right, 1, 1) for right in row] for row in rights]
    news = []
    for whole, right, left in zip(wholes, rights, lefts):
        rows = len(whole)
        down = [flow(whole[r + 1] - whole[r]) for r in range(rows - 1)]
        new = []
        for r in range(rows):
            total = right[r] - left[r]
            if r > 0:
                total = total - down[r - 1]
            if r + 1 < rows:
                total = total + down[r]
            new.append(whole[r] + time_step * total)
        news.append(new)
    return news


def map_kernel(turns, parts, local_kb, first, *refs):
    count = len(turns)
    refs = list(refs)
    changes = [refs.pop(0) for _ in range(parts)]
    coefs = [refs.pop(0) for _ in range(parts)]
    if not first:
        refs.pop(0)
    out_ref, grids, staged, sem = refs
    rows = grids.shape[0]
    height = count * local_kb
    top = turns[0] * local_kb
    before = jnp.concatenate([ref[top : top + height, :] for ref in coefs], axis=1)
    values = jnp.concatenate([before, jnp.concatenate([ref[...] for ref in changes], axis=1)], axis=0)
    depth, half = TURNS * local_kb, TILE_ROWS // 2
    where = [ref[depth:, :].astype(jnp.float32) for ref in coefs]
    row = jnp.concatenate([value[:1] for value in where], axis=1)
    lane = jnp.concatenate([value[half : half + 1] for value in where], axis=1)
    targets = (row * MAP_W + lane).astype(jnp.int32)
    pair = 2 if rows % 2 == 0 else 1
    pixel = lax.broadcasted_iota(jnp.int32, (pair * MAP_W, targets.shape[1]), 0)
    for r in range(0, rows, pair):
        chosen = jnp.where(pixel == targets - r * MAP_W, 2.0, 0.0).astype(jnp.bfloat16)
        moved = lax.dot_general(
            values, chosen, (((1,), (1,)), ((), ())), preferred_element_type=jnp.float32
        )
        total = moved[:height] + moved[height:]
        for i in range(pair):
            grids[r + i] = total[:, i * MAP_W : (i + 1) * MAP_W]
    groups = height // SUBLANES
    together = UNROLL if groups % UNROLL == 0 and rows * UNROLL <= 32 else 1
    chunk = together * SUBLANES * rows
    start = turns[0] * local_kb * rows

    def one(step, carry):
        wholes = []
        for i in range(together):
            at = pl.multiple_of((step * together + i) * SUBLANES, SUBLANES)
            wholes.append([grids[r, pl.ds(at, SUBLANES), :] for r in range(rows)])
        for _ in range(SWEEPS):
            wholes = spread(wholes)
        at = step * chunk
        for i, whole in enumerate(wholes):
            for r in range(rows):
                staged[pl.ds(at + i * SUBLANES * rows + r, SUBLANES, stride=rows), :] = 0.5 * whole[r]
        pltpu.make_async_copy(
            staged.at[pl.ds(pl.multiple_of(at, chunk), chunk)],
            out_ref.at[pl.ds(pl.multiple_of(start + at, chunk), chunk)],
            sem,
        ).start()
        return carry

    lax.fori_loop(0, groups // together, one, 0)
    pltpu.make_async_copy(staged, out_ref.at[pl.ds(start, height * rows)], sem).wait()


def run_maps(turns, changes, coefs, buffer):
    parts = len(changes)
    count, points = len(turns), changes[0].shape[1]
    local_kb = changes[0].shape[0] // count
    rows = parts * points // MAP_W
    first = buffer is None
    height = count * local_kb
    extra = [] if first else [buffer]
    return pl.pallas_call(
        functools.partial(map_kernel, turns, parts, local_kb, first),
        out_shape=jax.ShapeDtypeStruct((TURNS * local_kb * rows, MAP_W), jnp.float32),
        in_specs=[VMEM] * (2 * parts) + [ANY] * len(extra),
        out_specs=ANY,
        scratch_shapes=[
            pltpu.VMEM((rows, height, MAP_W), jnp.float32),
            pltpu.VMEM((height * rows, MAP_W), jnp.float32),
            pltpu.SemaphoreType.DMA,
        ],
        input_output_aliases={} if first else {2 * parts: 0},
        cost_estimate=pl.CostEstimate(
            flops=4 * height * (parts * points) ** 2,
            bytes_accessed=8 * height * parts * points,
            transcendentals=0,
        ),
        compiler_params=pltpu.CompilerParams(vmem_limit_bytes=GRANT),
    )(*changes, *coefs, *extra)


def exchange(value, axis, size, distance):
    return lax.ppermute(value, axis, [(i, i ^ distance) for i in range(size)])


def hop(turn, k):
    low = k & -k
    high = 1 << (k.bit_length() - 1)
    return high if turn % 2 == 0 else low


def per_device(fields, parts, residual_in, coefs_in, dictionary, owner_order, pixel_of):
    residual = residual_in[0]
    points = residual.shape[0]
    coefs = coefs_in[0].reshape(points, -1)
    chips = fields // 2
    over_chips = lambda value, k: exchange(value, "field", fields, 2 * k)
    over_cores = lambda value: exchange(value, "field", fields, 1)
    over_points = lambda value, m: exchange(value, "point", parts, m)

    keep, give = cut_block(dictionary, chips)
    got = [over_cores(give[k]) for k in range(chips)]
    same = [keep[0]] + [over_chips(keep[k], k) for k in range(1, chips)]
    other = [got[0]] + [over_chips(got[k], k) for k in range(1, chips)]
    laid, turned = lay_coefs(coefs, pixel_of.reshape(1, points), parts)
    laid = [laid[0]] + [over_points(laid[m], m) for m in range(1, parts)]
    chosen = pick_turns(owner_order, same, other)

    def gather(turn):
        held = [chosen[turn]]
        for k in range(1, chips):
            bit = hop(turn, k)
            held.append(over_chips(held[k ^ bit], bit))
        return held + [over_cores(value) for value in held]

    buffer = None
    for turns in GROUPS:
        pieces = [gather(turn) for turn in turns]
        residual, sends = run_turns(turns, residual, turned, pieces, parts)
        changes = [sends[0]] + [over_points(sends[m], m) for m in range(1, parts)]
        buffer = run_maps(turns, changes, laid, buffer)
    rows = parts * points // MAP_W
    return buffer.reshape(1, TURNS, -1, rows, MAP_W)


def wrapped(fields, parts, *args):
    return per_device(fields, parts, *args)


def solution(mesh):
    placed = (
        P("field", "point", None),
        P("field", "point", None, None),
        P("field", None),
        P(),
        P("field", "point"),
    )
    fields, parts = mesh.shape["field"], mesh.shape["point"]
    return jax.shard_map(
        functools.partial(wrapped, fields, parts),
        mesh=mesh,
        in_specs=placed,
        out_specs=P("field", None, "point", None, None),
        check_vma=False,
    )
```

```python
import functools

import jax
import jax.numpy as jnp
from jax import lax
from jax.experimental import pallas as pl
from jax.experimental.pallas import tpu as pltpu
from jax.sharding import PartitionSpec as P


TURNS = 4
SWEEPS = 4
MAP_W = 128
SUBLANES = 8
UNROLL = 8
TILE_ROWS = 16
GRANT = 16 * 1024 * 1024


time_step = 0.2

GROUPS = ((0, 1), (2, 3))

ANY = pl.BlockSpec(memory_space=pl.ANY)
VMEM = pl.BlockSpec(memory_space=pltpu.VMEM)
SMEM = pl.BlockSpec(memory_space=pltpu.SMEM)


def place_of_device():
    index = lax.axis_index("field")
    return index // 2, index % 2


def hops(turn, chips):
    bits = [1 << i for i in range(chips.bit_length() - 1)]
    return bits if turn % 2 == 0 else bits[::-1]


def distances(turn, chips):
    found = [0]
    for bit in hops(turn, chips):
        found += [bit ^ k for k in found]
    return found


def slice_kernel(chips, block_ref, *refs):
    keep, give = refs[:chips], refs[chips:]
    chip, core = place_of_device()
    rows, half = keep[0].shape
    for k in range(chips):
        top = pl.multiple_of((chip ^ k) * rows, rows)
        for out, which in ((keep[k], core), (give[k], 1 - core)):
            left = pl.multiple_of(which * half, half)
            out[...] = block_ref[pl.ds(top, rows), pl.ds(left, half)]


def cut_block(block, chips):
    kb, features = block.shape
    piece = jax.ShapeDtypeStruct((kb // chips, features // 2), block.dtype)
    outs = pl.pallas_call(
        functools.partial(slice_kernel, chips),
        out_shape=[piece] * (2 * chips),
        in_specs=[VMEM],
        out_specs=[VMEM] * (2 * chips),
        compiler_params=pltpu.CompilerParams(vmem_limit_bytes=GRANT),
        name="cut",
    )(block)
    return outs[:chips], outs[chips:]


def pick_kernel(chips, order_ref, *refs):
    pieces, outs = refs[: 2 * chips], refs[2 * chips :]
    chip, core = place_of_device()
    for turn in range(TURNS):
        owner = order_ref[turn]
        wanted = ((owner // 2) ^ chip) + chips * ((owner % 2) ^ core)
        for number, piece in enumerate(pieces):

            @pl.when(wanted == number)
            def _():
                outs[turn][...] = piece[...]


def pick_turns(owner_order, same, other):
    chips = len(same)
    piece = jax.ShapeDtypeStruct(same[0].shape, same[0].dtype)
    return pl.pallas_call(
        functools.partial(pick_kernel, chips),
        out_shape=[piece] * TURNS,
        in_specs=[SMEM] + [VMEM] * (2 * chips),
        out_specs=[VMEM] * TURNS,
        compiler_params=pltpu.CompilerParams(vmem_limit_bytes=GRANT),
        name="pick",
    )(owner_order, *same, *other)


def lay_kernel(parts, coefs_ref, pixel_ref, *refs):
    sends, turned = refs[:parts], refs[parts]
    slot = lax.axis_index("point")
    height, points = sends[0].shape
    local_kb = (height - TILE_ROWS) // TURNS
    turned[...] = coefs_ref[...].astype(jnp.float32).T.astype(jnp.bfloat16)
    pixel = pixel_ref[...]
    half = TILE_ROWS // 2
    row = jnp.broadcast_to((pixel // MAP_W).astype(jnp.float32), (half, points))
    lane = jnp.broadcast_to((pixel % MAP_W).astype(jnp.float32), (half, points))
    both = jnp.concatenate([row, lane], axis=0).astype(jnp.bfloat16)
    for m in range(parts):
        for turn in range(TURNS):
            top = pl.multiple_of((turn * parts + (slot ^ m)) * local_kb, local_kb)
            sends[m][turn * local_kb : (turn + 1) * local_kb, :] = turned[pl.ds(top, local_kb), :]
        sends[m][TURNS * local_kb :, :] = both


def lay_coefs(coefs, pixels, parts):
    points, width = coefs.shape
    send = jax.ShapeDtypeStruct((width // parts + TILE_ROWS, points), jnp.bfloat16)
    outs = pl.pallas_call(
        functools.partial(lay_kernel, parts),
        out_shape=[send] * parts + [jax.ShapeDtypeStruct((width, points), jnp.bfloat16)],
        in_specs=[VMEM, VMEM],
        out_specs=[VMEM] * (parts + 1),
        compiler_params=pltpu.CompilerParams(vmem_limit_bytes=GRANT),
        name="lay",
    )(coefs, pixels)
    return outs[:parts], outs[parts]


def turn_kernel(turns, chips, parts, last, *refs):
    refs = list(refs)
    residual_ref, coefs_ref = refs.pop(0), refs.pop(0)
    number = 1 + len(hops(0, chips))
    pieces = [[[refs.pop(0) for _ in range(number)] for _ in range(2)] for _ in turns]
    residual_out = None if last else refs.pop(0)
    sends = [refs.pop(0) for _ in range(parts)]
    values, held = refs

    chip, core = place_of_device()
    slot = lax.axis_index("point")
    rows, half = pieces[0][0][0].shape
    kb = rows * chips
    local_kb = kb // parts
    sides = [pl.ds(pl.multiple_of(which * half, half), half) for which in (core, 1 - core)]
    across = lambda left, right: lax.dot_general(
        left, right, (((1,), (1,)), ((), ())), preferred_element_type=jnp.float32
    )

    source = residual_ref
    for position, turn in enumerate(turns):
        tops = [pl.multiple_of((chip ^ k) * rows, rows) for k in distances(turn, chips)]
        halves = [jnp.concatenate([piece[...] for piece in side], axis=0) for side in pieces[position]]
        gram = across(halves[0], halves[0]) + across(halves[1], halves[1])
        step = 1.0 / jnp.sum(jnp.abs(gram), axis=1, keepdims=True)
        correlation = across(halves[0], source[:, sides[0]]) + across(halves[1], source[:, sides[1]])
        before = jnp.concatenate(
            [coefs_ref[pl.ds(pl.multiple_of(turn * kb + top, rows), rows), :] for top in tops], axis=0
        ).astype(jnp.float32)
        after = jnp.maximum(before + step * correlation, 0.0)
        change = (after - before).astype(jnp.bfloat16)
        for k in range(chips):
            values[pl.ds(tops[k], rows), :] = change[k * rows : (k + 1) * rows, :]
        if turn + 1 < TURNS:
            target = residual_out if position + 1 == len(turns) else held
            for side, part in zip(sides, halves):
                moved = lax.dot_general(
                    change, part, (((0,), (0,)), ((), ())), preferred_element_type=jnp.float32
                )
                target[:, side] = (source[:, side].astype(jnp.float32) - moved).astype(jnp.bfloat16)
            source = target
        for m in range(parts):
            top = pl.multiple_of((slot ^ m) * local_kb, local_kb)
            sends[m][position * local_kb : (position + 1) * local_kb, :] = values[
                pl.ds(top, local_kb), :
            ]


def run_turns(turns, chips, residual, coefs, pieces, parts):
    count = len(turns)
    last = turns[-1] + 1 == TURNS
    points, features = residual.shape
    kb = coefs.shape[0] // TURNS
    send = jax.ShapeDtypeStruct((count * kb // parts, points), jnp.bfloat16)
    flat = [piece for turn in pieces for side in turn for piece in side]
    first = [] if last else [jax.ShapeDtypeStruct(residual.shape, residual.dtype)]
    flops = count * 2 * kb * features * (kb + 2 * points)
    outs = pl.pallas_call(
        functools.partial(turn_kernel, turns, chips, parts, last),
        out_shape=first + [send] * parts,
        in_specs=[VMEM] * (2 + len(flat)),
        out_specs=[VMEM] * (len(first) + parts),
        scratch_shapes=[
            pltpu.VMEM((kb, points), jnp.bfloat16),
            pltpu.VMEM(residual.shape, residual.dtype),
        ],
        cost_estimate=pl.CostEstimate(
            flops=flops, bytes_accessed=2 * features * (2 * points + count * kb), transcendentals=0
        ),
        compiler_params=pltpu.CompilerParams(vmem_limit_bytes=GRANT),
    )(residual, coefs, *flat)
    outs = list(outs)
    return (None if last else outs.pop(0)), outs


def spread(wholes):
    lane = lax.broadcasted_iota(jnp.int32, wholes[0][0].shape, 1)
    inner = lane < MAP_W - 1

    def flow(differ):
        return differ / (1.0 + differ * differ)

    shifted = [[pltpu.roll(row, MAP_W - 1, 1) for row in whole] for whole in wholes]
    rights = [
        [jnp.where(inner, flow(right - row), 0.0) for row, right in zip(whole, moved)]
        for whole, moved in zip(wholes, shifted)
    ]
    lefts = [[pltpu.roll(right, 1, 1) for right in row] for row in rights]
    news = []
    for whole, right, left in zip(wholes, rights, lefts):
        rows = len(whole)
        down = [flow(whole[r + 1] - whole[r]) for r in range(rows - 1)]
        new = []
        for r in range(rows):
            total = right[r] - left[r]
            if r > 0:
                total = total - down[r - 1]
            if r + 1 < rows:
                total = total + down[r]
            new.append(whole[r] + time_step * total)
        news.append(new)
    return news


def targets_of(coefs):
    half = TILE_ROWS // 2
    depth = coefs[0].shape[0] - TILE_ROWS
    where = [ref[depth:, :].astype(jnp.float32) for ref in coefs]
    row = jnp.concatenate([value[:1] for value in where], axis=1)
    lane = jnp.concatenate([value[half : half + 1] for value in where], axis=1)
    return (row * MAP_W + lane).astype(jnp.int32)


def place(values, targets, rows, put):
    pair = 2 if rows % 2 == 0 else 1
    pixel = lax.broadcasted_iota(jnp.int32, (pair * MAP_W, targets.shape[1]), 0)
    for r in range(0, rows, pair):
        chosen = jnp.where(pixel == targets - r * MAP_W, 2.0, 0.0).astype(jnp.bfloat16)
        moved = lax.dot_general(
            values, chosen, (((1,), (1,)), ((), ())), preferred_element_type=jnp.float32
        )
        for i in range(pair):
            put(r + i, moved[:, i * MAP_W : (i + 1) * MAP_W])


def place_kernel(*refs):
    coefs, base = refs[:-1], refs[-1]
    depth = coefs[0].shape[0] - TILE_ROWS
    values = jnp.concatenate([ref[:depth, :] for ref in coefs], axis=1)

    def put(r, value):
        base[r] = value

    place(values, targets_of(coefs), base.shape[0], put)


def place_coefs(coefs):
    rows = len(coefs) * coefs[0].shape[1] // MAP_W
    depth = coefs[0].shape[0] - TILE_ROWS
    return pl.pallas_call(
        place_kernel,
        out_shape=jax.ShapeDtypeStruct((rows, depth, MAP_W), jnp.float32),
        in_specs=[VMEM] * len(coefs),
        out_specs=VMEM,
        cost_estimate=pl.CostEstimate(
            flops=2 * depth * (rows * MAP_W) ** 2, bytes_accessed=8 * depth * rows * MAP_W, transcendentals=0
        ),
        compiler_params=pltpu.CompilerParams(vmem_limit_bytes=GRANT),
        name="place",
    )(*coefs)


def map_kernel(turns, parts, local_kb, first, *refs):
    count = len(turns)
    refs = list(refs)
    changes = [refs.pop(0) for _ in range(parts)]
    coefs = [refs.pop(0) for _ in range(parts)]
    base = refs.pop(0)
    if not first:
        refs.pop(0)
    out_ref, grids, staged, sem = refs
    rows = grids.shape[0]
    height = count * local_kb
    top = turns[0] * local_kb

    def put(r, value):
        grids[r] = base[r, top : top + height, :] + value

    place(jnp.concatenate([ref[...] for ref in changes], axis=1), targets_of(coefs), rows, put)
    groups = height // SUBLANES
    together = UNROLL if groups % UNROLL == 0 and rows * UNROLL <= 64 else 1
    chunk = together * SUBLANES * rows
    start = turns[0] * local_kb * rows

    def one(step, carry):
        wholes = []
        for i in range(together):
            at = pl.multiple_of((step * together + i) * SUBLANES, SUBLANES)
            wholes.append([grids[r, pl.ds(at, SUBLANES), :] for r in range(rows)])
        for _ in range(SWEEPS):
            wholes = spread(wholes)
        at = step * chunk
        for i, whole in enumerate(wholes):
            for r in range(rows):
                staged[pl.ds(at + i * SUBLANES * rows + r, SUBLANES, stride=rows), :] = 0.5 * whole[r]
        pltpu.make_async_copy(
            staged.at[pl.ds(pl.multiple_of(at, chunk), chunk)],
            out_ref.at[pl.ds(pl.multiple_of(start + at, chunk), chunk)],
            sem,
        ).start()
        return carry

    lax.fori_loop(0, groups // together, one, 0)
    pltpu.make_async_copy(staged, out_ref.at[pl.ds(start, height * rows)], sem).wait()


def run_maps(turns, changes, coefs, base, buffer):
    parts = len(changes)
    count, points = len(turns), changes[0].shape[1]
    local_kb = changes[0].shape[0] // count
    rows = parts * points // MAP_W
    first = buffer is None
    height = count * local_kb
    extra = [] if first else [buffer]
    return pl.pallas_call(
        functools.partial(map_kernel, turns, parts, local_kb, first),
        out_shape=jax.ShapeDtypeStruct((TURNS * local_kb * rows, MAP_W), jnp.float32),
        in_specs=[VMEM] * (2 * parts + 1) + [ANY] * len(extra),
        out_specs=ANY,
        scratch_shapes=[
            pltpu.VMEM((rows, height, MAP_W), jnp.float32),
            pltpu.VMEM((height * rows, MAP_W), jnp.float32),
            pltpu.SemaphoreType.DMA,
        ],
        input_output_aliases={} if first else {2 * parts + 1: 0},
        cost_estimate=pl.CostEstimate(
            flops=2 * height * (parts * points) ** 2,
            bytes_accessed=8 * height * parts * points,
            transcendentals=0,
        ),
        compiler_params=pltpu.CompilerParams(vmem_limit_bytes=GRANT),
    )(*changes, *coefs, base, *extra)


def exchange(value, axis, size, distance):
    return lax.ppermute(value, axis, [(i, i ^ distance) for i in range(size)])


def per_device(fields, parts, residual_in, coefs_in, dictionary, owner_order, pixel_of):
    residual = residual_in[0]
    points = residual.shape[0]
    coefs = coefs_in[0].reshape(points, -1)
    chips = fields // 2
    over_chips = lambda value, k: exchange(value, "field", fields, 2 * k)
    over_cores = lambda value: exchange(value, "field", fields, 1)
    over_points = lambda value, m: exchange(value, "point", parts, m)

    keep, give = cut_block(dictionary, chips)
    got = [over_cores(give[k]) for k in range(chips)]
    same = [keep[0]] + [over_chips(keep[k], k) for k in range(1, chips)]
    other = [got[0]] + [over_chips(got[k], k) for k in range(1, chips)]
    laid, turned = lay_coefs(coefs, pixel_of.reshape(1, points), parts)
    laid = [laid[0]] + [over_points(laid[m], m) for m in range(1, parts)]
    base = place_coefs(laid)
    chosen = pick_turns(owner_order, same, other)

    def gather(turn):
        held = [chosen[turn]]
        for step, bit in enumerate(hops(turn, chips)):
            whole = held[0] if step == 0 else jnp.concatenate(held, axis=0)
            held.append(over_chips(whole, bit))
        return [held, [over_cores(value) for value in held]]

    buffer = None
    for turns in GROUPS:
        pieces = [gather(turn) for turn in turns]
        residual, sends = run_turns(turns, chips, residual, turned, pieces, parts)
        changes = [sends[0]] + [over_points(sends[m], m) for m in range(1, parts)]
        buffer = run_maps(turns, changes, laid, base, buffer)
    rows = parts * points // MAP_W
    return buffer.reshape(1, TURNS, -1, rows, MAP_W)


def wrapped(fields, parts, *args):
    return per_device(fields, parts, *args)


def solution(mesh):
    placed = (
        P("field", "point", None),
        P("field", "point", None, None),
        P("field", None),
        P(),
        P("field", "point"),
    )
    fields, parts = mesh.shape["field"], mesh.shape["point"]
    return jax.shard_map(
        functools.partial(wrapped, fields, parts),
        mesh=mesh,
        in_specs=placed,
        out_specs=P("field", None, "point", None, None),
        check_vma=False,
    )
```

```python
import functools

import jax
import jax.numpy as jnp
from jax import lax
from jax.experimental import pallas as pl
from jax.experimental.pallas import tpu as pltpu
from jax.sharding import PartitionSpec as P


TURNS = 4
SWEEPS = 4
MAP_W = 128
SUBLANES = 8
UNROLL = 8
TILE_ROWS = 16
SHARED_ROWS = 32
GRANT = 16 * 1024 * 1024


time_step = 0.2

GROUPS = ((0, 1), (2, 3))

ANY = pl.BlockSpec(memory_space=pl.ANY)
VMEM = pl.BlockSpec(memory_space=pltpu.VMEM)
SMEM = pl.BlockSpec(memory_space=pltpu.SMEM)


def place_of_device():
    index = lax.axis_index("field")
    return index // 2, index % 2


def hops(turn, chips):
    bits = [1 << i for i in range(chips.bit_length() - 1)]
    return bits if turn % 2 == 0 else bits[::-1]


def distances(turn, chips):
    found = [0]
    for bit in hops(turn, chips):
        found += [bit ^ k for k in found]
    return found


def spans(chips, rows):
    return [rows // 2 if k & (k - 1) and rows >= SHARED_ROWS else rows for k in range(chips)]


def slice_kernel(chips, block_ref, *refs):
    keep, give = refs[:chips], refs[chips:]
    chip, core = place_of_device()
    parity = lax.axis_index("point") % 2
    rows, half = give[0].shape
    for k in range(chips):
        for out, which in ((keep[k], core), (give[k], 1 - core)):
            span = out.shape[0]
            top = (chip ^ k) * rows + (0 if span == rows else parity * span)
            left = pl.multiple_of(which * half, half)
            out[...] = block_ref[pl.ds(pl.multiple_of(top, span), span), pl.ds(left, half)]


def cut_block(block, chips):
    kb, features = block.shape
    rows = kb // chips
    outs = pl.pallas_call(
        functools.partial(slice_kernel, chips),
        out_shape=[
            jax.ShapeDtypeStruct((span, features // 2), block.dtype) for span in spans(chips, rows) + [rows] * chips
        ],
        in_specs=[VMEM],
        out_specs=[VMEM] * (2 * chips),
        compiler_params=pltpu.CompilerParams(vmem_limit_bytes=GRANT),
        name="cut",
    )(block)
    return outs[:chips], outs[chips:]


def pick_kernel(turns, counts, order_ref, *refs):
    refs = list(refs)
    pieces = [[refs.pop(0) for _ in range(count)] for count in counts]
    chips = len(pieces) // 2
    chip, core = place_of_device()
    parity = lax.axis_index("point") % 2
    for position, turn in enumerate(turns):
        owner = order_ref[turn]
        wanted = ((owner // 2) ^ chip) + chips * ((owner % 2) ^ core)
        for number, piece in enumerate(pieces):

            @pl.when(wanted == number)
            def _():
                if len(piece) == 1:
                    refs[position][...] = piece[0][...]
                else:
                    span = piece[0].shape[0]
                    for part, which in zip(piece, (parity, 1 - parity)):
                        refs[position][pl.ds(pl.multiple_of(which * span, span), span), :] = part[...]


def pick_turns(turns, owner_order, pieces):
    flat = [part for piece in pieces for part in piece]
    piece = jax.ShapeDtypeStruct(pieces[0][0].shape, flat[0].dtype)
    return pl.pallas_call(
        functools.partial(pick_kernel, turns, [len(piece) for piece in pieces]),
        out_shape=[piece] * len(turns),
        in_specs=[SMEM] + [VMEM] * len(flat),
        out_specs=[VMEM] * len(turns),
        compiler_params=pltpu.CompilerParams(vmem_limit_bytes=GRANT),
    )(owner_order, *flat)


def lay_kernel(parts, coefs_ref, pixel_ref, *refs):
    sends, turned = refs[:parts], refs[parts]
    slot = lax.axis_index("point")
    height, points = sends[0].shape
    local_kb = (height - TILE_ROWS) // TURNS
    turned[...] = coefs_ref[...].astype(jnp.float32).T.astype(jnp.bfloat16)
    pixel = pixel_ref[...]
    half = TILE_ROWS // 2
    row = jnp.broadcast_to((pixel // MAP_W).astype(jnp.float32), (half, points))
    lane = jnp.broadcast_to((pixel % MAP_W).astype(jnp.float32), (half, points))
    both = jnp.concatenate([row, lane], axis=0).astype(jnp.bfloat16)
    for m in range(parts):
        for turn in range(TURNS):
            top = pl.multiple_of((turn * parts + (slot ^ m)) * local_kb, local_kb)
            sends[m][turn * local_kb : (turn + 1) * local_kb, :] = turned[pl.ds(top, local_kb), :]
        sends[m][TURNS * local_kb :, :] = both


def lay_coefs(coefs, pixels, parts):
    points, width = coefs.shape
    send = jax.ShapeDtypeStruct((width // parts + TILE_ROWS, points), jnp.bfloat16)
    outs = pl.pallas_call(
        functools.partial(lay_kernel, parts),
        out_shape=[send] * parts + [jax.ShapeDtypeStruct((width, points), jnp.bfloat16)],
        in_specs=[VMEM, VMEM],
        out_specs=[VMEM] * (parts + 1),
        compiler_params=pltpu.CompilerParams(vmem_limit_bytes=GRANT),
        name="lay",
    )(coefs, pixels)
    return outs[:parts], outs[parts]


def turn_kernel(turns, chips, parts, last, *refs):
    refs = list(refs)
    residual_ref, coefs_ref = refs.pop(0), refs.pop(0)
    number = 1 + len(hops(0, chips))
    pieces = [[[refs.pop(0) for _ in range(number)] for _ in range(2)] for _ in turns]
    residual_out = None if last else refs.pop(0)
    sends = [refs.pop(0) for _ in range(parts)]
    values, held = refs

    chip, core = place_of_device()
    slot = lax.axis_index("point")
    rows, half = pieces[0][0][0].shape
    kb = rows * chips
    local_kb = kb // parts
    sides = [pl.ds(pl.multiple_of(which * half, half), half) for which in (core, 1 - core)]
    across = lambda left, right: lax.dot_general(
        left, right, (((1,), (1,)), ((), ())), preferred_element_type=jnp.float32
    )

    source = residual_ref
    for position, turn in enumerate(turns):
        tops = [pl.multiple_of((chip ^ k) * rows, rows) for k in distances(turn, chips)]
        halves = [jnp.concatenate([piece[...] for piece in side], axis=0) for side in pieces[position]]
        correlation = across(halves[0], source[:, sides[0]]) + across(halves[1], source[:, sides[1]])
        gram = across(halves[0], halves[0]) + across(halves[1], halves[1])
        step = 1.0 / jnp.sum(jnp.abs(gram), axis=1, keepdims=True)
        before = jnp.concatenate(
            [coefs_ref[pl.ds(pl.multiple_of(turn * kb + top, rows), rows), :] for top in tops], axis=0
        ).astype(jnp.float32)
        after = jnp.maximum(before + step * correlation, 0.0)
        change = (after - before).astype(jnp.bfloat16)
        for k in range(chips):
            values[pl.ds(tops[k], rows), :] = change[k * rows : (k + 1) * rows, :]
        if turn + 1 < TURNS:
            target = residual_out if position + 1 == len(turns) else held
            for side, part in zip(sides, halves):
                moved = lax.dot_general(
                    change, part, (((0,), (0,)), ((), ())), preferred_element_type=jnp.float32
                )
                target[:, side] = (source[:, side].astype(jnp.float32) - moved).astype(jnp.bfloat16)
            source = target
        for m in range(parts):
            top = pl.multiple_of((slot ^ m) * local_kb, local_kb)
            sends[m][position * local_kb : (position + 1) * local_kb, :] = values[
                pl.ds(top, local_kb), :
            ]


def run_turns(turns, chips, residual, coefs, pieces, parts):
    count = len(turns)
    last = turns[-1] + 1 == TURNS
    points, features = residual.shape
    kb = coefs.shape[0] // TURNS
    send = jax.ShapeDtypeStruct((count * kb // parts, points), jnp.bfloat16)
    flat = [piece for turn in pieces for side in turn for piece in side]
    first = [] if last else [jax.ShapeDtypeStruct(residual.shape, residual.dtype)]
    flops = count * 2 * kb * features * (kb + 2 * points)
    outs = pl.pallas_call(
        functools.partial(turn_kernel, turns, chips, parts, last),
        out_shape=first + [send] * parts,
        in_specs=[VMEM] * (2 + len(flat)),
        out_specs=[VMEM] * (len(first) + parts),
        scratch_shapes=[
            pltpu.VMEM((kb, points), jnp.bfloat16),
            pltpu.VMEM(residual.shape, residual.dtype),
        ],
        cost_estimate=pl.CostEstimate(
            flops=flops, bytes_accessed=2 * features * (2 * points + count * kb), transcendentals=0
        ),
        compiler_params=pltpu.CompilerParams(vmem_limit_bytes=GRANT),
    )(residual, coefs, *flat)
    outs = list(outs)
    return (None if last else outs.pop(0)), outs


def spread(wholes):
    lane = lax.broadcasted_iota(jnp.int32, wholes[0][0].shape, 1)
    inner = lane < MAP_W - 1

    def flow(differ):
        return differ / (1.0 + differ * differ)

    shifted = [[pltpu.roll(row, MAP_W - 1, 1) for row in whole] for whole in wholes]
    rights = [
        [jnp.where(inner, flow(right - row), 0.0) for row, right in zip(whole, moved)]
        for whole, moved in zip(wholes, shifted)
    ]
    lefts = [[pltpu.roll(right, 1, 1) for right in row] for row in rights]
    news = []
    for whole, right, left in zip(wholes, rights, lefts):
        rows = len(whole)
        down = [flow(whole[r + 1] - whole[r]) for r in range(rows - 1)]
        new = []
        for r in range(rows):
            total = right[r] - left[r]
            if r > 0:
                total = total - down[r - 1]
            if r + 1 < rows:
                total = total + down[r]
            new.append(whole[r] + time_step * total)
        news.append(new)
    return news


def targets_of(coefs):
    half = TILE_ROWS // 2
    depth = coefs[0].shape[0] - TILE_ROWS
    where = [ref[depth:, :].astype(jnp.float32) for ref in coefs]
    row = jnp.concatenate([value[:1] for value in where], axis=1)
    lane = jnp.concatenate([value[half : half + 1] for value in where], axis=1)
    return (row * MAP_W + lane).astype(jnp.int32)


def place(values, targets, rows, put):
    pair = 2 if rows % 2 == 0 else 1
    pixel = lax.broadcasted_iota(jnp.int32, (pair * MAP_W, targets.shape[1]), 0)
    for r in range(0, rows, pair):
        chosen = jnp.where(pixel == targets - r * MAP_W, 2.0, 0.0).astype(jnp.bfloat16)
        moved = lax.dot_general(
            values, chosen, (((1,), (1,)), ((), ())), preferred_element_type=jnp.float32
        )
        for i in range(pair):
            put(r + i, moved[:, i * MAP_W : (i + 1) * MAP_W])


def place_kernel(*refs):
    coefs, base = refs[:-1], refs[-1]
    depth = coefs[0].shape[0] - TILE_ROWS
    values = jnp.concatenate([ref[:depth, :] for ref in coefs], axis=1)

    def put(r, value):
        base[r] = value

    place(values, targets_of(coefs), base.shape[0], put)


def place_coefs(coefs):
    rows = len(coefs) * coefs[0].shape[1] // MAP_W
    depth = coefs[0].shape[0] - TILE_ROWS
    return pl.pallas_call(
        place_kernel,
        out_shape=jax.ShapeDtypeStruct((rows, depth, MAP_W), jnp.float32),
        in_specs=[VMEM] * len(coefs),
        out_specs=VMEM,
        cost_estimate=pl.CostEstimate(
            flops=2 * depth * (rows * MAP_W) ** 2, bytes_accessed=8 * depth * rows * MAP_W, transcendentals=0
        ),
        compiler_params=pltpu.CompilerParams(vmem_limit_bytes=GRANT),
        name="place",
    )(*coefs)


def map_kernel(turns, parts, local_kb, first, *refs):
    count = len(turns)
    refs = list(refs)
    changes = [refs.pop(0) for _ in range(parts)]
    coefs = [refs.pop(0) for _ in range(parts)]
    base = refs.pop(0)
    if not first:
        refs.pop(0)
    out_ref, grids, staged, sem = refs
    rows = grids.shape[0]
    height = count * local_kb
    top = turns[0] * local_kb

    def put(r, value):
        grids[r] = base[r, top : top + height, :] + value

    place(jnp.concatenate([ref[...] for ref in changes], axis=1), targets_of(coefs), rows, put)
    groups = height // SUBLANES
    together = UNROLL if groups % UNROLL == 0 and rows * UNROLL <= 64 else 1
    chunk = together * SUBLANES * rows
    start = turns[0] * local_kb * rows

    def one(step, carry):
        wholes = []
        for i in range(together):
            at = pl.multiple_of((step * together + i) * SUBLANES, SUBLANES)
            wholes.append([grids[r, pl.ds(at, SUBLANES), :] for r in range(rows)])
        for _ in range(SWEEPS):
            wholes = spread(wholes)
        at = step * chunk
        for i, whole in enumerate(wholes):
            for r in range(rows):
                staged[pl.ds(at + i * SUBLANES * rows + r, SUBLANES, stride=rows), :] = 0.5 * whole[r]
        pltpu.make_async_copy(
            staged.at[pl.ds(pl.multiple_of(at, chunk), chunk)],
            out_ref.at[pl.ds(pl.multiple_of(start + at, chunk), chunk)],
            sem,
        ).start()
        return carry

    lax.fori_loop(0, groups // together, one, 0, unroll=groups // together <= 2)
    pltpu.make_async_copy(staged, out_ref.at[pl.ds(start, height * rows)], sem).wait()


def run_maps(turns, changes, coefs, base, buffer):
    parts = len(changes)
    count, points = len(turns), changes[0].shape[1]
    local_kb = changes[0].shape[0] // count
    rows = parts * points // MAP_W
    first = buffer is None
    height = count * local_kb
    extra = [] if first else [buffer]
    return pl.pallas_call(
        functools.partial(map_kernel, turns, parts, local_kb, first),
        out_shape=jax.ShapeDtypeStruct((TURNS * local_kb * rows, MAP_W), jnp.float32),
        in_specs=[VMEM] * (2 * parts + 1) + [ANY] * len(extra),
        out_specs=ANY,
        scratch_shapes=[
            pltpu.VMEM((rows, height, MAP_W), jnp.float32),
            pltpu.VMEM((height * rows, MAP_W), jnp.float32),
            pltpu.SemaphoreType.DMA,
        ],
        input_output_aliases={} if first else {2 * parts + 1: 0},
        cost_estimate=pl.CostEstimate(
            flops=2 * height * (parts * points) ** 2,
            bytes_accessed=8 * height * parts * points,
            transcendentals=0,
        ),
        compiler_params=pltpu.CompilerParams(vmem_limit_bytes=GRANT),
    )(*changes, *coefs, base, *extra)


def exchange(value, axis, size, distance):
    return lax.ppermute(value, axis, [(i, i ^ distance) for i in range(size)])


def per_device(fields, parts, residual_in, coefs_in, dictionary, owner_order, pixel_of):
    residual = residual_in[0]
    points = residual.shape[0]
    coefs = coefs_in[0].reshape(points, -1)
    chips = fields // 2
    over_chips = lambda value, k: exchange(value, "field", fields, 2 * k)
    over_cores = lambda value: exchange(value, "field", fields, 1)
    over_points = lambda value, m: exchange(value, "point", parts, m)

    keep, give = cut_block(dictionary, chips)
    got = [over_cores(give[k]) for k in range(chips)]
    same = [[keep[0]]] + [[over_chips(keep[k], k)] for k in range(1, chips)]
    for k, piece in enumerate(same):
        if keep[k].shape != keep[0].shape:
            piece.append(over_points(piece[0], 1))
    other = [[got[0]]] + [[over_chips(got[k], k)] for k in range(1, chips)]
    laid, turned = lay_coefs(coefs, pixel_of.reshape(1, points), parts)
    laid = [laid[0]] + [over_points(laid[m], m) for m in range(1, parts)]
    base = place_coefs(laid)
    chosen = [piece for turns in GROUPS for piece in pick_turns(turns, owner_order, same + other)]

    def gather(turn):
        held = [chosen[turn]]
        for step, bit in enumerate(hops(turn, chips)):
            whole = held[0] if step == 0 else jnp.concatenate(held, axis=0)
            held.append(over_chips(whole, bit))
        return [held, [over_cores(value) for value in held]]

    buffer = None
    for turns in GROUPS:
        pieces = [gather(turn) for turn in turns]
        residual, sends = run_turns(turns, chips, residual, turned, pieces, parts)
        changes = [sends[0]] + [over_points(sends[m], m) for m in range(1, parts)]
        buffer = run_maps(turns, changes, laid, base, buffer)
    rows = parts * points // MAP_W
    return buffer.reshape(1, TURNS, -1, rows, MAP_W)


def wrapped(fields, parts, *args):
    return per_device(fields, parts, *args)


def solution(mesh):
    placed = (
        P("field", "point", None),
        P("field", "point", None, None),
        P("field", None),
        P(),
        P("field", "point"),
    )
    fields, parts = mesh.shape["field"], mesh.shape["point"]
    return jax.shard_map(
        functools.partial(wrapped, fields, parts),
        mesh=mesh,
        in_specs=placed,
        out_specs=P("field", None, "point", None, None),
        check_vma=False,
    )
```

```python
import functools

import jax
import jax.numpy as jnp
from jax import lax
from jax.experimental import pallas as pl
from jax.experimental.pallas import tpu as pltpu
from jax.sharding import PartitionSpec as P


TURNS = 4
SWEEPS = 4
MAP_W = 128
SUBLANES = 8
UNROLL = 16
TILE_ROWS = 16
GRANT = 16 * 1024 * 1024


time_step = 0.2

GROUPS = ((0, 1), (2, 3))

ANY = pl.BlockSpec(memory_space=pl.ANY)
VMEM = pl.BlockSpec(memory_space=pltpu.VMEM)
SMEM = pl.BlockSpec(memory_space=pltpu.SMEM)


def place_of_device():
    index = lax.axis_index("field")
    return index // 2, index % 2


def hops(turn, chips):
    bits = [1 << i for i in range(chips.bit_length() - 1)]
    return bits if turn % 2 == 0 else bits[::-1]


def distances(turn, chips):
    found = [0]
    for bit in hops(turn, chips):
        found += [bit ^ k for k in found]
    return found


def slice_kernel(chips, block_ref, *refs):
    keep, give = refs[:chips], refs[chips:]
    chip, core = place_of_device()
    rows, half = keep[0].shape
    for k in range(chips):
        top = pl.multiple_of((chip ^ k) * rows, rows)
        for out, which in ((keep[k], core), (give[k], 1 - core)):
            left = pl.multiple_of(which * half, half)
            out[...] = block_ref[pl.ds(top, rows), pl.ds(left, half)]


def cut_block(block, chips):
    kb, features = block.shape
    piece = jax.ShapeDtypeStruct((kb // chips, features // 2), block.dtype)
    outs = pl.pallas_call(
        functools.partial(slice_kernel, chips),
        out_shape=[piece] * (2 * chips),
        in_specs=[VMEM],
        out_specs=[VMEM] * (2 * chips),
        compiler_params=pltpu.CompilerParams(vmem_limit_bytes=GRANT),
        name="cut",
    )(block)
    return outs[:chips], outs[chips:]


def pick_kernel(turns, chips, order_ref, *refs):
    pieces, outs = refs[: 2 * chips], refs[2 * chips :]
    chip, core = place_of_device()
    for position, turn in enumerate(turns):
        owner = order_ref[turn]
        wanted = ((owner // 2) ^ chip) + chips * ((owner % 2) ^ core)
        for number, piece in enumerate(pieces):

            @pl.when(wanted == number)
            def _():
                outs[position][...] = piece[...]


def pick_turns(turns, owner_order, same, other):
    chips = len(same)
    piece = jax.ShapeDtypeStruct(same[0].shape, same[0].dtype)
    return pl.pallas_call(
        functools.partial(pick_kernel, turns, chips),
        out_shape=[piece] * len(turns),
        in_specs=[SMEM] + [VMEM] * (2 * chips),
        out_specs=[VMEM] * len(turns),
        compiler_params=pltpu.CompilerParams(vmem_limit_bytes=GRANT),
    )(owner_order, *same, *other)


def lay_kernel(parts, coefs_ref, pixel_ref, *refs):
    sends, turned = refs[:parts], refs[parts]
    slot = lax.axis_index("point")
    height, points = sends[0].shape
    local_kb = (height - TILE_ROWS) // TURNS
    turned[...] = coefs_ref[...].astype(jnp.float32).T.astype(jnp.bfloat16)
    pixel = pixel_ref[...]
    half = TILE_ROWS // 2
    row = jnp.broadcast_to((pixel // MAP_W).astype(jnp.float32), (half, points))
    lane = jnp.broadcast_to((pixel % MAP_W).astype(jnp.float32), (half, points))
    both = jnp.concatenate([row, lane], axis=0).astype(jnp.bfloat16)
    for m in range(parts):
        for turn in range(TURNS):
            top = pl.multiple_of((turn * parts + (slot ^ m)) * local_kb, local_kb)
            sends[m][turn * local_kb : (turn + 1) * local_kb, :] = turned[pl.ds(top, local_kb), :]
        sends[m][TURNS * local_kb :, :] = both


def lay_coefs(coefs, pixels, parts):
    points, width = coefs.shape
    send = jax.ShapeDtypeStruct((width // parts + TILE_ROWS, points), jnp.bfloat16)
    outs = pl.pallas_call(
        functools.partial(lay_kernel, parts),
        out_shape=[send] * parts + [jax.ShapeDtypeStruct((width, points), jnp.bfloat16)],
        in_specs=[VMEM, VMEM],
        out_specs=[VMEM] * (parts + 1),
        compiler_params=pltpu.CompilerParams(vmem_limit_bytes=GRANT),
        name="lay",
    )(coefs, pixels)
    return outs[:parts], outs[parts]


def turn_kernel(turns, chips, parts, last, *refs):
    refs = list(refs)
    residual_ref, coefs_ref = refs.pop(0), refs.pop(0)
    number = 1 + len(hops(0, chips))
    pieces = [[[refs.pop(0) for _ in range(number)] for _ in range(2)] for _ in turns]
    residual_out = None if last else refs.pop(0)
    sends = [refs.pop(0) for _ in range(parts)]
    values, held = refs

    chip, core = place_of_device()
    slot = lax.axis_index("point")
    rows, half = pieces[0][0][0].shape
    kb = rows * chips
    local_kb = kb // parts
    sides = [pl.ds(pl.multiple_of(which * half, half), half) for which in (core, 1 - core)]
    across = lambda left, right: lax.dot_general(
        left, right, (((1,), (1,)), ((), ())), preferred_element_type=jnp.float32
    )

    source = residual_ref
    for position, turn in enumerate(turns):
        tops = [pl.multiple_of((chip ^ k) * rows, rows) for k in distances(turn, chips)]
        halves = [jnp.concatenate([piece[...] for piece in side], axis=0) for side in pieces[position]]
        correlation = across(halves[0], source[:, sides[0]]) + across(halves[1], source[:, sides[1]])
        gram = across(halves[0], halves[0]) + across(halves[1], halves[1])
        step = 1.0 / jnp.sum(jnp.abs(gram), axis=1, keepdims=True)
        before = jnp.concatenate(
            [coefs_ref[pl.ds(pl.multiple_of(turn * kb + top, rows), rows), :] for top in tops], axis=0
        ).astype(jnp.float32)
        after = jnp.maximum(before + step * correlation, 0.0)
        change = (after - before).astype(jnp.bfloat16)
        for k in range(chips):
            values[pl.ds(tops[k], rows), :] = change[k * rows : (k + 1) * rows, :]
        if turn + 1 < TURNS:
            target = residual_out if position + 1 == len(turns) else held
            for side, part in zip(sides, halves):
                moved = lax.dot_general(
                    change, part, (((0,), (0,)), ((), ())), preferred_element_type=jnp.float32
                )
                target[:, side] = (source[:, side].astype(jnp.float32) - moved).astype(jnp.bfloat16)
            source = target
        for m in range(parts):
            top = pl.multiple_of((slot ^ m) * local_kb, local_kb)
            sends[m][position * local_kb : (position + 1) * local_kb, :] = values[
                pl.ds(top, local_kb), :
            ]


def run_turns(turns, chips, residual, coefs, pieces, parts):
    count = len(turns)
    last = turns[-1] + 1 == TURNS
    points, features = residual.shape
    kb = coefs.shape[0] // TURNS
    send = jax.ShapeDtypeStruct((count * kb // parts, points), jnp.bfloat16)
    flat = [piece for turn in pieces for side in turn for piece in side]
    first = [] if last else [jax.ShapeDtypeStruct(residual.shape, residual.dtype)]
    flops = count * 2 * kb * features * (kb + 2 * points)
    outs = pl.pallas_call(
        functools.partial(turn_kernel, turns, chips, parts, last),
        out_shape=first + [send] * parts,
        in_specs=[VMEM] * (2 + len(flat)),
        out_specs=[VMEM] * (len(first) + parts),
        scratch_shapes=[
            pltpu.VMEM((kb, points), jnp.bfloat16),
            pltpu.VMEM(residual.shape, residual.dtype),
        ],
        cost_estimate=pl.CostEstimate(
            flops=flops, bytes_accessed=2 * features * (2 * points + count * kb), transcendentals=0
        ),
        compiler_params=pltpu.CompilerParams(vmem_limit_bytes=GRANT),
    )(residual, coefs, *flat)
    outs = list(outs)
    return (None if last else outs.pop(0)), outs


def spread(wholes):
    lane = lax.broadcasted_iota(jnp.int32, wholes[0][0].shape, 1)
    inner = lane < MAP_W - 1

    def flow(differ):
        return differ / (1.0 + differ * differ)

    shifted = [[pltpu.roll(row, MAP_W - 1, 1) for row in whole] for whole in wholes]
    rights = [
        [jnp.where(inner, flow(right - row), 0.0) for row, right in zip(whole, moved)]
        for whole, moved in zip(wholes, shifted)
    ]
    lefts = [[pltpu.roll(right, 1, 1) for right in row] for row in rights]
    news = []
    for whole, right, left in zip(wholes, rights, lefts):
        rows = len(whole)
        down = [flow(whole[r + 1] - whole[r]) for r in range(rows - 1)]
        new = []
        for r in range(rows):
            total = right[r] - left[r]
            if r > 0:
                total = total - down[r - 1]
            if r + 1 < rows:
                total = total + down[r]
            new.append(whole[r] + time_step * total)
        news.append(new)
    return news


def targets_of(coefs):
    half = TILE_ROWS // 2
    depth = coefs[0].shape[0] - TILE_ROWS
    where = [ref[depth:, :].astype(jnp.float32) for ref in coefs]
    row = jnp.concatenate([value[:1] for value in where], axis=1)
    lane = jnp.concatenate([value[half : half + 1] for value in where], axis=1)
    return (row * MAP_W + lane).astype(jnp.int32)


def place(values, targets, rows, put):
    pair = 2 if rows % 2 == 0 else 1
    pixel = lax.broadcasted_iota(jnp.int32, (pair * MAP_W, targets.shape[1]), 0)
    for r in range(0, rows, pair):
        chosen = jnp.where(pixel == targets - r * MAP_W, 2.0, 0.0).astype(jnp.bfloat16)
        moved = lax.dot_general(
            values, chosen, (((1,), (1,)), ((), ())), preferred_element_type=jnp.float32
        )
        for i in range(pair):
            put(r + i, moved[:, i * MAP_W : (i + 1) * MAP_W])


def place_kernel(*refs):
    coefs, base = refs[:-1], refs[-1]
    depth = coefs[0].shape[0] - TILE_ROWS
    values = jnp.concatenate([ref[:depth, :] for ref in coefs], axis=1)

    def put(r, value):
        base[r] = value

    place(values, targets_of(coefs), base.shape[0], put)


def place_coefs(coefs):
    rows = len(coefs) * coefs[0].shape[1] // MAP_W
    depth = coefs[0].shape[0] - TILE_ROWS
    return pl.pallas_call(
        place_kernel,
        out_shape=jax.ShapeDtypeStruct((rows, depth, MAP_W), jnp.float32),
        in_specs=[VMEM] * len(coefs),
        out_specs=VMEM,
        cost_estimate=pl.CostEstimate(
            flops=2 * depth * (rows * MAP_W) ** 2, bytes_accessed=8 * depth * rows * MAP_W, transcendentals=0
        ),
        compiler_params=pltpu.CompilerParams(vmem_limit_bytes=GRANT),
        name="place",
    )(*coefs)


def map_kernel(turns, parts, local_kb, first, *refs):
    count = len(turns)
    refs = list(refs)
    changes = [refs.pop(0) for _ in range(parts)]
    coefs = [refs.pop(0) for _ in range(parts)]
    base = refs.pop(0)
    if not first:
        refs.pop(0)
    out_ref, grids, staged, sem = refs
    rows = grids.shape[0]
    height = count * local_kb
    top = turns[0] * local_kb

    def put(r, value):
        grids[r] = base[r, top : top + height, :] + value

    place(jnp.concatenate([ref[...] for ref in changes], axis=1), targets_of(coefs), rows, put)
    groups = height // SUBLANES
    together = UNROLL if groups % UNROLL == 0 and rows * UNROLL <= 128 else 1
    chunk = together * SUBLANES * rows
    start = turns[0] * local_kb * rows

    def one(step, carry):
        wholes = []
        for i in range(together):
            at = pl.multiple_of((step * together + i) * SUBLANES, SUBLANES)
            wholes.append([grids[r, pl.ds(at, SUBLANES), :] for r in range(rows)])
        for _ in range(SWEEPS):
            wholes = spread(wholes)
        at = step * chunk
        for i, whole in enumerate(wholes):
            for r in range(rows):
                staged[pl.ds(at + i * SUBLANES * rows + r, SUBLANES, stride=rows), :] = 0.5 * whole[r]
        pltpu.make_async_copy(
            staged.at[pl.ds(pl.multiple_of(at, chunk), chunk)],
            out_ref.at[pl.ds(pl.multiple_of(start + at, chunk), chunk)],
            sem,
        ).start()
        return carry

    lax.fori_loop(0, groups // together, one, 0)
    pltpu.make_async_copy(staged, out_ref.at[pl.ds(start, height * rows)], sem).wait()


def run_maps(turns, changes, coefs, base, buffer):
    parts = len(changes)
    count, points = len(turns), changes[0].shape[1]
    local_kb = changes[0].shape[0] // count
    rows = parts * points // MAP_W
    first = buffer is None
    height = count * local_kb
    extra = [] if first else [buffer]
    return pl.pallas_call(
        functools.partial(map_kernel, turns, parts, local_kb, first),
        out_shape=jax.ShapeDtypeStruct((TURNS * local_kb * rows, MAP_W), jnp.float32),
        in_specs=[VMEM] * (2 * parts + 1) + [ANY] * len(extra),
        out_specs=ANY,
        scratch_shapes=[
            pltpu.VMEM((rows, height, MAP_W), jnp.float32),
            pltpu.VMEM((height * rows, MAP_W), jnp.float32),
            pltpu.SemaphoreType.DMA,
        ],
        input_output_aliases={} if first else {2 * parts + 1: 0},
        cost_estimate=pl.CostEstimate(
            flops=2 * height * (parts * points) ** 2,
            bytes_accessed=8 * height * parts * points,
            transcendentals=0,
        ),
        compiler_params=pltpu.CompilerParams(vmem_limit_bytes=GRANT),
    )(*changes, *coefs, base, *extra)


def exchange(value, axis, size, distance):
    return lax.ppermute(value, axis, [(i, i ^ distance) for i in range(size)])


def per_device(fields, parts, residual_in, coefs_in, dictionary, owner_order, pixel_of):
    residual = residual_in[0]
    points = residual.shape[0]
    coefs = coefs_in[0].reshape(points, -1)
    chips = fields // 2
    over_chips = lambda value, k: exchange(value, "field", fields, 2 * k)
    over_cores = lambda value: exchange(value, "field", fields, 1)
    over_points = lambda value, m: exchange(value, "point", parts, m)

    keep, give = cut_block(dictionary, chips)
    got = [over_cores(give[k]) for k in range(chips)]
    same = [keep[0]] + [over_chips(keep[k], k) for k in range(1, chips)]
    other = [got[0]] + [over_chips(got[k], k) for k in range(1, chips)]
    laid, turned = lay_coefs(coefs, pixel_of.reshape(1, points), parts)
    laid = [laid[0]] + [over_points(laid[m], m) for m in range(1, parts)]
    base = place_coefs(laid)
    chosen = [piece for turns in GROUPS for piece in pick_turns(turns, owner_order, same, other)]

    def gather(turn):
        held = [chosen[turn]]
        for step, bit in enumerate(hops(turn, chips)):
            whole = held[0] if step == 0 else jnp.concatenate(held, axis=0)
            held.append(over_chips(whole, bit))
        return [held, [over_cores(value) for value in held]]

    buffer = None
    for turns in GROUPS:
        pieces = [gather(turn) for turn in turns]
        residual, sends = run_turns(turns, chips, residual, turned, pieces, parts)
        changes = [sends[0]] + [over_points(sends[m], m) for m in range(1, parts)]
        buffer = run_maps(turns, changes, laid, base, buffer)
    rows = parts * points // MAP_W
    return buffer.reshape(1, TURNS, -1, rows, MAP_W)


def wrapped(fields, parts, *args):
    return per_device(fields, parts, *args)


def solution(mesh):
    placed = (
        P("field", "point", None),
        P("field", "point", None, None),
        P("field", None),
        P(),
        P("field", "point"),
    )
    fields, parts = mesh.shape["field"], mesh.shape["point"]
    return jax.shard_map(
        functools.partial(wrapped, fields, parts),
        mesh=mesh,
        in_specs=placed,
        out_specs=P("field", None, "point", None, None),
        check_vma=False,
    )
```

```python
import functools

import jax
import jax.numpy as jnp
from jax import lax
from jax.experimental import pallas as pl
from jax.experimental.pallas import tpu as pltpu
from jax.sharding import PartitionSpec as P


TURNS = 4
SWEEPS = 4
MAP_W = 128
SUBLANES = 8
UNROLL = 8
TILE_ROWS = 16
GRANT = 16 * 1024 * 1024


time_step = 0.2

GROUPS = ((0, 1), (2, 3))

ANY = pl.BlockSpec(memory_space=pl.ANY)
VMEM = pl.BlockSpec(memory_space=pltpu.VMEM)
SMEM = pl.BlockSpec(memory_space=pltpu.SMEM)


def place_of_device():
    index = lax.axis_index("field")
    return index // 2, index % 2


def hops(turn, chips):
    bits = [1 << i for i in range(chips.bit_length() - 1)]
    return bits if turn % 2 == 0 else bits[::-1]


def distances(turn, chips):
    found = [0]
    for bit in hops(turn, chips):
        found += [bit ^ k for k in found]
    return found


def slice_kernel(chips, block_ref, *refs):
    keep, give = refs[:chips], refs[chips:]
    chip, core = place_of_device()
    rows, half = keep[0].shape
    for k in range(chips):
        top = pl.multiple_of((chip ^ k) * rows, rows)
        for out, which in ((keep[k], core), (give[k], 1 - core)):
            left = pl.multiple_of(which * half, half)
            out[...] = block_ref[pl.ds(top, rows), pl.ds(left, half)]


def cut_block(block, chips):
    kb, features = block.shape
    piece = jax.ShapeDtypeStruct((kb // chips, features // 2), block.dtype)
    outs = pl.pallas_call(
        functools.partial(slice_kernel, chips),
        out_shape=[piece] * (2 * chips),
        in_specs=[VMEM],
        out_specs=[VMEM] * (2 * chips),
        compiler_params=pltpu.CompilerParams(vmem_limit_bytes=GRANT),
        name="cut",
    )(block)
    return outs[:chips], outs[chips:]


def pick_kernel(turns, chips, order_ref, *refs):
    pieces, outs = refs[: 2 * chips], refs[2 * chips :]
    chip, core = place_of_device()
    for position, turn in enumerate(turns):
        owner = order_ref[turn]
        wanted = ((owner // 2) ^ chip) + chips * ((owner % 2) ^ core)
        for number, piece in enumerate(pieces):

            @pl.when(wanted == number)
            def _():
                outs[position][...] = piece[...]


def pick_turns(turns, owner_order, same, other):
    chips = len(same)
    piece = jax.ShapeDtypeStruct(same[0].shape, same[0].dtype)
    return pl.pallas_call(
        functools.partial(pick_kernel, turns, chips),
        out_shape=[piece] * len(turns),
        in_specs=[SMEM] + [VMEM] * (2 * chips),
        out_specs=[VMEM] * len(turns),
        compiler_params=pltpu.CompilerParams(vmem_limit_bytes=GRANT),
    )(owner_order, *same, *other)


def lay_kernel(parts, coefs_ref, pixel_ref, *refs):
    sends, turned = refs[:parts], refs[parts]
    slot = lax.axis_index("point")
    height, points = sends[0].shape
    local_kb = (height - TILE_ROWS) // TURNS
    turned[...] = coefs_ref[...].astype(jnp.float32).T.astype(jnp.bfloat16)
    pixel = pixel_ref[...]
    half = TILE_ROWS // 2
    row = jnp.broadcast_to((pixel // MAP_W).astype(jnp.float32), (half, points))
    lane = jnp.broadcast_to((pixel % MAP_W).astype(jnp.float32), (half, points))
    both = jnp.concatenate([row, lane], axis=0).astype(jnp.bfloat16)
    for m in range(parts):
        for turn in range(TURNS):
            top = pl.multiple_of((turn * parts + (slot ^ m)) * local_kb, local_kb)
            sends[m][turn * local_kb : (turn + 1) * local_kb, :] = turned[pl.ds(top, local_kb), :]
        sends[m][TURNS * local_kb :, :] = both


def lay_coefs(coefs, pixels, parts):
    points, width = coefs.shape
    send = jax.ShapeDtypeStruct((width // parts + TILE_ROWS, points), jnp.bfloat16)
    outs = pl.pallas_call(
        functools.partial(lay_kernel, parts),
        out_shape=[send] * parts + [jax.ShapeDtypeStruct((width, points), jnp.bfloat16)],
        in_specs=[VMEM, VMEM],
        out_specs=[VMEM] * (parts + 1),
        compiler_params=pltpu.CompilerParams(vmem_limit_bytes=GRANT),
        name="lay",
    )(coefs, pixels)
    return outs[:parts], outs[parts]


def turn_kernel(turns, chips, parts, last, *refs):
    refs = list(refs)
    residual_ref, coefs_ref = refs.pop(0), refs.pop(0)
    number = 1 + len(hops(0, chips))
    pieces = [[[refs.pop(0) for _ in range(number)] for _ in range(2)] for _ in turns]
    residual_out = None if last else refs.pop(0)
    sends = [refs.pop(0) for _ in range(parts)]
    values, held = refs

    chip, core = place_of_device()
    slot = lax.axis_index("point")
    rows, half = pieces[0][0][0].shape
    kb = rows * chips
    local_kb = kb // parts
    sides = [pl.ds(pl.multiple_of(which * half, half), half) for which in (core, 1 - core)]
    across = lambda left, right: lax.dot_general(
        left, right, (((1,), (1,)), ((), ())), preferred_element_type=jnp.float32
    )

    source = residual_ref
    for position, turn in enumerate(turns):
        tops = [pl.multiple_of((chip ^ k) * rows, rows) for k in distances(turn, chips)]
        halves = [jnp.concatenate([piece[...] for piece in side], axis=0) for side in pieces[position]]
        correlation = across(halves[0], source[:, sides[0]]) + across(halves[1], source[:, sides[1]])
        gram = across(halves[0], halves[0]) + across(halves[1], halves[1])
        step = 1.0 / jnp.sum(jnp.abs(gram), axis=1, keepdims=True)
        before = jnp.concatenate(
            [coefs_ref[pl.ds(pl.multiple_of(turn * kb + top, rows), rows), :] for top in tops], axis=0
        ).astype(jnp.float32)
        after = jnp.maximum(before + step * correlation, 0.0)
        change = (after - before).astype(jnp.bfloat16)
        for k in range(chips):
            values[pl.ds(tops[k], rows), :] = change[k * rows : (k + 1) * rows, :]
        if turn + 1 < TURNS:
            target = residual_out if position + 1 == len(turns) else held
            for side, part in zip(sides, halves):
                moved = lax.dot_general(
                    change, part, (((0,), (0,)), ((), ())), preferred_element_type=jnp.float32
                )
                target[:, side] = (source[:, side].astype(jnp.float32) - moved).astype(jnp.bfloat16)
            source = target
        for m in range(parts):
            top = pl.multiple_of((slot ^ m) * local_kb, local_kb)
            sends[m][position * local_kb : (position + 1) * local_kb, :] = values[
                pl.ds(top, local_kb), :
            ]


def run_turns(turns, chips, residual, coefs, pieces, parts):
    count = len(turns)
    last = turns[-1] + 1 == TURNS
    points, features = residual.shape
    kb = coefs.shape[0] // TURNS
    send = jax.ShapeDtypeStruct((count * kb // parts, points), jnp.bfloat16)
    flat = [piece for turn in pieces for side in turn for piece in side]
    first = [] if last else [jax.ShapeDtypeStruct(residual.shape, residual.dtype)]
    flops = count * 2 * kb * features * (kb + 2 * points)
    outs = pl.pallas_call(
        functools.partial(turn_kernel, turns, chips, parts, last),
        out_shape=first + [send] * parts,
        in_specs=[VMEM] * (2 + len(flat)),
        out_specs=[VMEM] * (len(first) + parts),
        scratch_shapes=[
            pltpu.VMEM((kb, points), jnp.bfloat16),
            pltpu.VMEM(residual.shape, residual.dtype),
        ],
        cost_estimate=pl.CostEstimate(
            flops=flops, bytes_accessed=2 * features * (2 * points + count * kb), transcendentals=0
        ),
        compiler_params=pltpu.CompilerParams(vmem_limit_bytes=GRANT),
    )(residual, coefs, *flat)
    outs = list(outs)
    return (None if last else outs.pop(0)), outs


def spread(wholes):
    lane = lax.broadcasted_iota(jnp.int32, wholes[0][0].shape, 1)
    inner = lane < MAP_W - 1

    def flow(differ):
        return differ / (1.0 + differ * differ)

    shifted = [[pltpu.roll(row, MAP_W - 1, 1) for row in whole] for whole in wholes]
    rights = [
        [jnp.where(inner, flow(right - row), 0.0) for row, right in zip(whole, moved)]
        for whole, moved in zip(wholes, shifted)
    ]
    lefts = [[pltpu.roll(right, 1, 1) for right in row] for row in rights]
    news = []
    for whole, right, left in zip(wholes, rights, lefts):
        rows = len(whole)
        down = [flow(whole[r + 1] - whole[r]) for r in range(rows - 1)]
        new = []
        for r in range(rows):
            total = right[r] - left[r]
            if r > 0:
                total = total - down[r - 1]
            if r + 1 < rows:
                total = total + down[r]
            new.append(whole[r] + time_step * total)
        news.append(new)
    return news


def targets_of(coefs):
    half = TILE_ROWS // 2
    depth = coefs[0].shape[0] - TILE_ROWS
    where = [ref[depth:, :].astype(jnp.float32) for ref in coefs]
    row = jnp.concatenate([value[:1] for value in where], axis=1)
    lane = jnp.concatenate([value[half : half + 1] for value in where], axis=1)
    return (row * MAP_W + lane).astype(jnp.int32)


def place(values, targets, rows, put):
    pair = 2 if rows % 2 == 0 else 1
    pixel = lax.broadcasted_iota(jnp.int32, (pair * MAP_W, targets.shape[1]), 0)
    for r in range(0, rows, pair):
        chosen = jnp.where(pixel == targets - r * MAP_W, 2.0, 0.0).astype(jnp.bfloat16)
        moved = lax.dot_general(
            values, chosen, (((1,), (1,)), ((), ())), preferred_element_type=jnp.float32
        )
        for i in range(pair):
            put(r + i, moved[:, i * MAP_W : (i + 1) * MAP_W])


def place_kernel(*refs):
    coefs, base = refs[:-1], refs[-1]
    depth = coefs[0].shape[0] - TILE_ROWS
    values = jnp.concatenate([ref[:depth, :] for ref in coefs], axis=1)

    def put(r, value):
        base[r] = value

    place(values, targets_of(coefs), base.shape[0], put)


def place_coefs(coefs):
    rows = len(coefs) * coefs[0].shape[1] // MAP_W
    depth = coefs[0].shape[0] - TILE_ROWS
    return pl.pallas_call(
        place_kernel,
        out_shape=jax.ShapeDtypeStruct((rows, depth, MAP_W), jnp.float32),
        in_specs=[VMEM] * len(coefs),
        out_specs=VMEM,
        cost_estimate=pl.CostEstimate(
            flops=2 * depth * (rows * MAP_W) ** 2, bytes_accessed=8 * depth * rows * MAP_W, transcendentals=0
        ),
        compiler_params=pltpu.CompilerParams(vmem_limit_bytes=GRANT),
        name="place",
    )(*coefs)


def map_kernel(turns, parts, local_kb, first, *refs):
    count = len(turns)
    refs = list(refs)
    changes = [refs.pop(0) for _ in range(parts)]
    coefs = [refs.pop(0) for _ in range(parts)]
    base = refs.pop(0)
    if not first:
        refs.pop(0)
    out_ref, grids, staged, sem = refs
    rows = grids.shape[0]
    height = count * local_kb
    top = turns[0] * local_kb

    def put(r, value):
        grids[r] = base[r, top : top + height, :] + value

    place(jnp.concatenate([ref[...] for ref in changes], axis=1), targets_of(coefs), rows, put)
    groups = height // SUBLANES
    together = UNROLL if groups % UNROLL == 0 and rows * UNROLL <= 64 else 1
    chunk = together * SUBLANES * rows
    start = turns[0] * local_kb * rows

    def one(step, carry):
        wholes = []
        for i in range(together):
            at = pl.multiple_of((step * together + i) * SUBLANES, SUBLANES)
            wholes.append([grids[r, pl.ds(at, SUBLANES), :] for r in range(rows)])
        for _ in range(SWEEPS):
            wholes = spread(wholes)
        at = step * chunk
        for i, whole in enumerate(wholes):
            for r in range(rows):
                staged[pl.ds(at + i * SUBLANES * rows + r, SUBLANES, stride=rows), :] = 0.5 * whole[r]
        pltpu.make_async_copy(
            staged.at[pl.ds(pl.multiple_of(at, chunk), chunk)],
            out_ref.at[pl.ds(pl.multiple_of(start + at, chunk), chunk)],
            sem,
        ).start()
        return carry

    lax.fori_loop(0, groups // together, one, 0, unroll=groups // together <= 2)
    pltpu.make_async_copy(staged, out_ref.at[pl.ds(start, height * rows)], sem).wait()


def run_maps(turns, changes, coefs, base, buffer):
    parts = len(changes)
    count, points = len(turns), changes[0].shape[1]
    local_kb = changes[0].shape[0] // count
    rows = parts * points // MAP_W
    first = buffer is None
    height = count * local_kb
    extra = [] if first else [buffer]
    return pl.pallas_call(
        functools.partial(map_kernel, turns, parts, local_kb, first),
        out_shape=jax.ShapeDtypeStruct((TURNS * local_kb * rows, MAP_W), jnp.float32),
        in_specs=[VMEM] * (2 * parts + 1) + [ANY] * len(extra),
        out_specs=ANY,
        scratch_shapes=[
            pltpu.VMEM((rows, height, MAP_W), jnp.float32),
            pltpu.VMEM((height * rows, MAP_W), jnp.float32),
            pltpu.SemaphoreType.DMA,
        ],
        input_output_aliases={} if first else {2 * parts + 1: 0},
        cost_estimate=pl.CostEstimate(
            flops=2 * height * (parts * points) ** 2,
            bytes_accessed=8 * height * parts * points,
            transcendentals=0,
        ),
        compiler_params=pltpu.CompilerParams(vmem_limit_bytes=GRANT),
    )(*changes, *coefs, base, *extra)


def exchange(value, axis, size, distance):
    return lax.ppermute(value, axis, [(i, i ^ distance) for i in range(size)])


def per_device(fields, parts, residual_in, coefs_in, dictionary, owner_order, pixel_of):
    residual = residual_in[0]
    points = residual.shape[0]
    coefs = coefs_in[0].reshape(points, -1)
    chips = fields // 2
    over_chips = lambda value, k: exchange(value, "field", fields, 2 * k)
    over_cores = lambda value: exchange(value, "field", fields, 1)
    over_points = lambda value, m: exchange(value, "point", parts, m)

    keep, give = cut_block(dictionary, chips)
    got = [over_cores(give[k]) for k in range(chips)]
    same = [keep[0]] + [over_chips(keep[k], k) for k in range(1, chips)]
    other = [got[0]] + [over_chips(got[k], k) for k in range(1, chips)]
    laid, turned = lay_coefs(coefs, pixel_of.reshape(1, points), parts)
    laid = [laid[0]] + [over_points(laid[m], m) for m in range(1, parts)]
    base = place_coefs(laid)
    chosen = [piece for turns in GROUPS for piece in pick_turns(turns, owner_order, same, other)]

    def gather(turn):
        held = [chosen[turn]]
        for step, bit in enumerate(hops(turn, chips)):
            whole = held[0] if step == 0 else jnp.concatenate(held, axis=0)
            held.append(over_chips(whole, bit))
        return [held, [over_cores(value) for value in held]]

    buffer = None
    for turns in GROUPS:
        pieces = [gather(turn) for turn in turns]
        residual, sends = run_turns(turns, chips, residual, turned, pieces, parts)
        changes = [sends[0]] + [over_points(sends[m], m) for m in range(1, parts)]
        buffer = run_maps(turns, changes, laid, base, buffer)
    rows = parts * points // MAP_W
    return buffer.reshape(1, TURNS, -1, rows, MAP_W)


def wrapped(fields, parts, *args):
    return per_device(fields, parts, *args)


def solution(mesh):
    placed = (
        P("field", "point", None),
        P("field", "point", None, None),
        P("field", None),
        P(),
        P("field", "point"),
    )
    fields, parts = mesh.shape["field"], mesh.shape["point"]
    return jax.shard_map(
        functools.partial(wrapped, fields, parts),
        mesh=mesh,
        in_specs=placed,
        out_specs=P("field", None, "point", None, None),
        check_vma=False,
    )
```
